128 devices in a mesh: fem: 8 (over y, core), bem: 16 (over z, x).
Axes of the slice: x: 4, y: 4, z: 4, core: 2. Of those that a mesh axis runs over, the one named last changes fastest.
Arguments:
- fem_field: float32 [4, 1048576], P(None, ('fem', 'bem')), may hold values from -6 to 6
- elem_mats: float32 [4, 4, 4194304], P(None, None, ('fem', 'bem')), may hold values from -1.8 to 1.8
- elem_nodes: int32 [4, 4194304], P(None, ('fem', 'bem')), may hold values from 0 to 9215
- trace_count: int32 [128], P(('fem', 'bem')), may hold values from 1 to 16384, 1572864 in all
- trace_node: int32 [2097152], P(('fem', 'bem')), may hold values from 0 to 8191
- trace_block: int32 [2097152, 1], P(('fem', 'bem')), may hold values from 0 to 127; in each aligned block of 16384 rows (0 to 16383, 16384 to 32767, ...) at most 256 rows name the same one
- trace_pos: int32 [2097152], P(('fem', 'bem')), may hold values from 0 to 1151
- trace_weight: float32 [2097152], P(('fem', 'bem')), may hold values from 0.2 to 1
- near_tiles: bfloat16 [16, 72, 128, 128], P('bem', 'fem'), may hold values from -0.5 to 0.5
- left_basis: bfloat16 [16, 16, 32, 9216], P('bem', None, None, 'fem'), may hold values from -0.0625 to 0.0625
- right_basis: bfloat16 [16, 16, 32, 9216], P('bem', None, None, 'fem'), may hold values from -0.375 to 0.375
- bem_field: float32 [16, 4, 9216], P('bem', None, 'fem'), may hold values from -6 to 6
Outputs:
- fem_out: float32 [4, 1048576], P(None, ('fem', 'bem'))
- bem_flux: float32 [16, 4, 9216], P('bem', None, 'fem')
The draws below stay inside these ranges and needn't reach their ends.
Inputs may be any that keep to these rules, and one draw needn't show every extreme that they name: `trace_block`: among the 16384 rows of one partition no BEM block is named by more than 256 rows, and some block is named by exactly 256 rows. `trace_count`: rows of a partition at or beyond its count are padding; some partition has 16384 live rows.
All inputs are finite; a program needn't handle non-finite values. No bound on the sum of `trace_count` on one device may be relied on, other than what follows from the above.
Results may differ from the reference program's by a relative error of at most 0.0003.
Values sent between devices are 32-bit elements; how exact they have to be, the bound alone decides.
A program may use at most 192 MiB of HBM per device.

```python
import math
import jax
import jax.numpy as jnp
import numpy as np
from jax import lax

RHS = 4
NODE_DEV = 8192
REACH = 512
TR_DEV = 16384
SUB = 1152
TILE = 128
RANK = 32
PARTITIONS = 128
ELEM_DEV = 32768
CAP = 256
SLICES = 16
SLICE = 9216
NTILE = 72
UNKNOWNS = 147456
NODES = 1048576
ELEMS = 4194304
TRACES = 2097152


def set_ends(values, stream_key, least, top_value):
    place = [jax.random.randint(jax.random.fold_in(stream_key, axis), (), 0, length) for axis, length in enumerate(values.shape)]
    widest = values.shape.index(max(values.shape))
    beside = place[:widest] + [(place[widest] + 1) % values.shape[widest]] + place[widest + 1:]
    return values.at[tuple(place)].set(least).at[tuple(beside)].set(top_value)


def with_spikes(result, stream_key, source, target, parts, factor):
    def block_of(position):
        return (jnp.arange(result.shape[position]) // (result.shape[position] // parts)).reshape((-1,) + (1,) * (result.ndim - 1 - position))

    near = jax.random.permutation(stream_key, parts)[block_of(target)]
    far = (block_of(target) + parts // 2) % parts
    return jnp.where((block_of(source) == near) | (block_of(source) == far), factor * result, result)


def shard_levels(rng, dims, cuts, least, top_value):
    loudness = 1.0
    for position, parts in cuts:
        steps = jax.random.uniform(jax.random.fold_in(jax.random.fold_in(rng, 6), position), (parts,), jnp.float32, least / len(cuts), top_value / len(cuts))
        loudness = loudness * jnp.repeat(jnp.exp(steps), dims[position] // parts).reshape((-1,) + (1,) * (len(dims) - 1 - position))
    return loudness


def profile(amount, total, reach, lean):
    portions = [(1 << 20) // math.isqrt(rank ** lean) + 1 for rank in range(2, amount + 1)]
    surplus, holding = total - reach - (amount - 1), [1] * (amount - 1)
    while surplus > 0:
        free = [i for i in range(amount - 1) if holding[i] < reach]
        pool, left = sum([portions[i] for i in free]), surplus
        for i in free:
            addition = min(reach - holding[i], max(1, left * portions[i] // pool), surplus)
            holding[i] = holding[i] + addition
            surplus = surplus - addition
    return np.array([reach] + holding)


def ragged(rng, count, total, bound, skew):
    if count == 2:
        one = jax.random.randint(rng, (), max(1, total - bound), min(bound, total - 1) + 1)
        return jnp.stack([one, total - one])
    sizes = jnp.asarray(profile(count, total, bound, skew), jnp.int32)
    pairs = (count - 1) // 2
    giver, sink = sizes[1:1 + 2 * pairs:2], sizes[2:2 + 2 * pairs:2]
    slack = jnp.minimum(giver - 1, bound - sink)
    moved = jax.random.randint(jax.random.fold_in(rng, 1), (pairs,), 0, 1 << 20) % (slack + 1)
    sizes = sizes.at[1:1 + 2 * pairs:2].set(giver - moved).at[2:2 + 2 * pairs:2].set(sink + moved)
    return sizes[jax.random.permutation(jax.random.fold_in(rng, 2), count)]


def deal_out(stream_key, own, number, rows, amount, top, bound, slope):
    order = jax.random.permutation(stream_key, amount)
    crowded, usual = portions_of(amount, rows * top, bound, slope, True), portions_of(amount, rows * top, bound, slope, False)
    places = jnp.arange(amount)

    def named(tallies, rotation):
        used = int((tallies > 0).sum())
        fixed = max(1, used // 4)
        moved = fixed + (places - fixed + rotation * (used - fixed)) % max(1, amount - fixed)
        return jnp.zeros((amount,), jnp.int32).at[order[jnp.where(places < fixed, places, moved)]].set(jnp.asarray(tallies, jnp.int32))

    tallies = jnp.where(number % 4 == 0, named(crowded, number // 4), named(usual, number - number // 4 - 1))
    mixed = jax.random.permutation(jax.random.fold_in(own, 3), amount)
    giver, sink = mixed[0:amount // 2 * 2:2], mixed[1:amount // 2 * 2:2]
    margin = jnp.minimum(tallies[giver] - 1, bound - tallies[sink]) // 2
    margin = jnp.where((giver == order[0]) | (sink == order[0]) | (tallies[sink] == 0), 0, jnp.maximum(margin, 0))
    moved = jax.random.randint(jax.random.fold_in(own, 4), (amount // 2,), 0, 1 << 20) % (margin + 1)
    tallies = tallies.at[giver].add(-moved).at[sink].add(moved)
    labels = jnp.searchsorted(jnp.cumsum(tallies), jnp.arange(rows * top), side="right").astype(jnp.int32)
    listing = labels.reshape(top, rows).T
    listing = listing[jax.random.permutation(jax.random.fold_in(own, 1), rows)]
    rotation = jax.random.randint(jax.random.fold_in(own, 2), (rows, 1), 0, top)
    return jnp.take_along_axis(listing, (jnp.arange(top)[None, :] + rotation) % top, axis=1)


def portions_of(number_of, total, bound, lean, full):
    portions = [(1 << 20) // math.isqrt(standing ** lean) + 1 for standing in range(1, number_of + 1)]
    largest = bound if full else min(bound, max(-(-total // number_of), total * portions[0] // sum(portions)))
    least = 1 if total - largest >= number_of - 1 else 0
    counts, rest = [largest] + [least] * (number_of - 1), total - largest - least * (number_of - 1)
    while rest > 0:
        candidates = [i for i in range(1, number_of) if counts[i] < largest] or [i for i in range(1, number_of) if counts[i] < bound]
        mass, budget = sum([portions[i] for i in candidates]), rest
        for i in candidates:
            more = min(bound - counts[i], max(1, budget * portions[i] // mass), rest)
            counts[i] = counts[i] + more
            rest = rest - more
    return np.array(counts)


def bell_draw(stream_key, shape, scale, most, split=(), kind=jnp.bfloat16):
    result = jax.random.normal(stream_key, shape, jnp.float32) * scale
    if len(split) > 0:
        result = shard_levels(stream_key, shape, split, -0.22, 0.18) * result
    return jnp.clip(result, min=-most, max=most).astype(kind)


def gaussian_with(rng, extent, deviation, bound, shards, heavy, kind=jnp.bfloat16):
    array = deviation * jax.random.normal(rng, extent, jnp.float32)
    if shards:
        array = array * shard_levels(rng, extent, shards, -0.22, 0.18)
    return jnp.clip(with_spikes(array, jax.random.fold_in(rng, 3), *heavy), -bound, bound).astype(kind)


def setup_inputs(seed: int = 0) -> dict:
    keys = jax.random.split(jax.random.key(seed), 13)
    fem_field = bell_draw(keys[0], (RHS, NODES), 1.0, 6.0, ((1, 128),), jnp.float32)
    elem_mats = bell_draw(keys[1], (4, 4, ELEMS), 0.3, 1.8, ((2, 128),), jnp.float32)
    elem_nodes = set_ends(jax.random.randint(keys[2], (4, ELEMS), 0, NODE_DEV + 2 * REACH), jax.random.fold_in(keys[2], 1), 0, (NODE_DEV + 2 * REACH) - 1).astype(jnp.int32)
    trace_count = ragged(keys[3], PARTITIONS, 3 * TR_DEV * PARTITIONS // 4, TR_DEV, 2).astype(jnp.int32)
    trace_node = set_ends(jax.random.randint(keys[4], (TRACES,), 0, NODE_DEV), jax.random.fold_in(keys[4], 1), 0, NODE_DEV - 1).astype(jnp.int32)
    trace_block_keys = jax.random.split(jax.random.fold_in(keys[5], 1), TRACES // TR_DEV)
    trace_block_turns = jax.random.permutation(jax.random.fold_in(keys[5], 3), TRACES // TR_DEV)
    trace_block = jax.vmap(lambda own, number: deal_out(jax.random.fold_in(keys[5], 2), own, number, TR_DEV, PARTITIONS, 1, CAP, 1))(trace_block_keys, trace_block_turns).reshape((TRACES, 1))
    trace_pos = set_ends(jax.random.randint(keys[6], (TRACES,), 0, SUB), jax.random.fold_in(keys[6], 1), 0, SUB - 1).astype(jnp.int32)
    trace_weight = jnp.clip(0.2 + 0.8 * jax.random.uniform(keys[7], (TRACES,), jnp.float32) ** shard_levels(keys[7], (TRACES,), ((0, 128),), -0.2, 0.2), 0.2, 1.0)
    near_tiles = bell_draw(keys[8], (SLICES, NTILE, TILE, TILE), TILE ** -0.5, 0.5, ((0, 16), (1, 8)))
    left_basis = bell_draw(keys[9], (SLICES, SLICES, RANK, SLICE), SLICE ** -0.5, 0.0625, ((0, 16), (3, 8)))
    right_basis = gaussian_with(keys[10], (SLICES, SLICES, RANK, SLICE), (RANK * SLICES) ** -0.5, 0.375, ((0, 16), (3, 8)), (0, 1, 16, 2.0))
    bem_field = bell_draw(keys[11], (SLICES, RHS, SLICE), 1.0, 6.0, ((0, 16), (2, 8)), jnp.float32)
    return dict(fem_field=fem_field, elem_mats=elem_mats, elem_nodes=elem_nodes, trace_count=trace_count, trace_node=trace_node, trace_block=trace_block, trace_pos=trace_pos, trace_weight=trace_weight, near_tiles=near_tiles, left_basis=left_basis, right_basis=right_basis, bem_field=bem_field)


def stiffness_apply(fem_field, elem_mats, elem_nodes):
    elem_part = jnp.arange(ELEMS, dtype=jnp.int32) // ELEM_DEV
    padded_index = (elem_part[None, :] * NODE_DEV + elem_nodes).astype(jnp.int32)
    padded = jnp.pad(fem_field, ((0, 0), (REACH, REACH)))
    corner = padded[:, padded_index]
    owned_mask = ((elem_nodes >= REACH) & (elem_nodes < REACH + NODE_DEV)).astype(fem_field.dtype)
    columns = []
    for column_at in range(4):
        summed = elem_mats[0, column_at][None, :] * corner[:, 0]
        for row_at in range(1, 4):
            summed = summed + elem_mats[row_at, column_at][None, :] * corner[:, row_at]
        columns.append(summed * owned_mask[column_at][None, :])
    contrib = jnp.stack(columns, axis=1)
    assembled = jnp.zeros((RHS, NODES + 2 * REACH), fem_field.dtype)
    assembled = assembled.at[:, padded_index.reshape(-1)].add(contrib.reshape(RHS, -1))
    return assembled[:, REACH:REACH + NODES]


def reference(fem_field, elem_mats, elem_nodes, trace_count, trace_node, trace_block, trace_pos, trace_weight, near_tiles, left_basis, right_basis, bem_field):
    stiffness = stiffness_apply(fem_field, elem_mats, elem_nodes)
    trace_rows = jnp.arange(TRACES, dtype=jnp.int32)
    trace_part = (trace_rows // TR_DEV).astype(jnp.int32)
    live_rows = (trace_rows - trace_part * TR_DEV) < trace_count[trace_part]
    trace_coef = jnp.where(live_rows, trace_weight, jnp.zeros_like(trace_weight))
    node_global = (trace_part * NODE_DEV + trace_node).astype(jnp.int32)
    unknown = (trace_block[:, 0] * SUB + trace_pos).astype(jnp.int32)
    values = fem_field[:, node_global] * trace_coef[None, :]
    traces = jnp.zeros((RHS, UNKNOWNS), fem_field.dtype).at[:, unknown].add(values)
    trace_wide = traces.reshape(RHS, SLICES, SLICE).transpose(1, 0, 2)

    def couple_one(inputs):
        basis_rows, slice_trace = inputs
        return jnp.einsum('cki,ri->crk', basis_rows.astype(slice_trace.dtype), slice_trace, precision=lax.Precision.HIGHEST)

    coupling = lax.map(couple_one, (left_basis, trace_wide))

    def far_column(slice_at):
        weights = lax.dynamic_index_in_dim(coupling, slice_at, axis=1, keepdims=False)
        basis_rows = lax.dynamic_index_in_dim(right_basis, slice_at, axis=1, keepdims=False)
        return jnp.einsum('srk,skj->rj', weights, basis_rows.astype(weights.dtype), precision=lax.Precision.HIGHEST)

    far_field = lax.map(far_column, jnp.arange(SLICES, dtype=jnp.int32))
    tiled_trace = trace_wide.reshape(SLICES, RHS, NTILE, TILE)
    near_field = jnp.einsum('ctiq,crti->crtq', near_tiles.astype(trace_wide.dtype), tiled_trace, precision=lax.Precision.HIGHEST).reshape(SLICES, RHS, SLICE)
    bem_flux = far_field + near_field + bem_field
    flux_flat = bem_flux.transpose(1, 0, 2).reshape(RHS, UNKNOWNS)
    returned = flux_flat[:, unknown] * trace_coef[None, :]
    fem_out = stiffness + jnp.zeros((RHS, NODES), fem_field.dtype).at[:, node_global].add(returned)
    return fem_out, bem_flux
```

```python
import functools

import jax
import jax.numpy as jnp
from jax import lax
from jax.experimental import pallas as pl
from jax.experimental.pallas import tpu as pltpu
from jax.sharding import PartitionSpec as P

REACH = 512
bf16 = jnp.bfloat16
f32 = jnp.float32
i32 = jnp.int32
MESH = pl.DeviceIdType.MESH
NT = (((1,), (1,)), ((), ()))
VMEM_LIMIT = 48 << 20


def iota(shape, dim):
    return lax.broadcasted_iota(i32, shape, dim)


def to_bf(x):
    return x.astype(f32).astype(bf16)


def onehot(rows, index):
    shape = (rows, index.shape[1])
    return jnp.where(
        to_bf(iota(shape, 0)) == jnp.broadcast_to(index, shape),
        jnp.ones((), bf16),
        jnp.zeros((), bf16),
    )


def split8(x):
    hi = x.astype(bf16).astype(f32)
    return jnp.where(iota(x.shape, 0) < 4, hi, x - hi)


def split_table(t):
    hi = t.astype(bf16)
    return jnp.concatenate([hi, (t - hi.astype(f32)).astype(bf16)], 1)


def pick(table, hot, q, groups):
    r = jnp.dot(table, jnp.concatenate([hot, hot], 0), preferred_element_type=f32)
    shape = (8, hot.shape[1])
    qh = jnp.broadcast_to(q, shape) - jnp.where(iota(shape, 0) >= 4, 1, 0)
    acc = jnp.where(qh == 0, r[0:8], 0.0)
    for j in range(1, groups):
        acc = jnp.where(qh == 2 * j, r[8 * j : 8 * j + 8], acc)
    return acc + pltpu.roll(acc, 4, axis=0)


def spread(part, q, groups):
    part = part.astype(bf16)
    p16 = jnp.concatenate([part, part], 0)
    qv = to_bf(jnp.broadcast_to(q, p16.shape) - jnp.where(iota(p16.shape, 0) >= 8, 1, 0))
    zero = jnp.zeros((), bf16)
    return jnp.concatenate(
        [jnp.where(qv == jnp.asarray(2 * j, bf16), p16, zero) for j in range(groups)], 0
    )


def first_step():
    return pl.program_id(0) == 0


def elem_kernel(t_ref, mats_ref, nodes_ref, out_ref, table):
    @pl.when(first_step())
    def _():
        out_ref[...] = jnp.zeros_like(out_ref)
        table[...] = split_table(t_ref[...])

    nodes = nodes_ref[...]
    hots, xs = [], []
    for a in range(4):
        n = nodes[a : a + 1]
        hot = onehot(256, to_bf(n & 255))
        hots.append(hot)
        xs.append(pick(table[...], hot, n >> 8, 18))
    total = None
    for b in range(4):
        c = mats_ref[pl.ds(b, 1), :] * xs[0]
        for a in range(1, 4):
            c = c + mats_ref[pl.ds(4 * a + b, 1), :] * xs[a]
        d = lax.dot_general(
            spread(split8(c), (nodes[b : b + 1] >> 8) - 2, 16),
            hots[b],
            NT,
            preferred_element_type=f32,
        )
        total = d if total is None else total + d
    out_ref[...] += total


def elem_call(table, mats, nodes):
    count = nodes.shape[1]
    eb = 512
    return pl.pallas_call(
        elem_kernel,
        grid=(count // eb,),
        in_specs=[
            pl.BlockSpec((144, 256), lambda i: (0, 0)),
            pl.BlockSpec((16, eb), lambda i: (0, i)),
            pl.BlockSpec((4, eb), lambda i: (0, i)),
        ],
        out_specs=pl.BlockSpec((256, 256), lambda i: (0, 0)),
        out_shape=jax.ShapeDtypeStruct((256, 256), f32),
        scratch_shapes=[pltpu.VMEM((144, 512), bf16)],
        compiler_params=pltpu.CompilerParams(vmem_limit_bytes=VMEM_LIMIT),
        name="elements",
    )(table, mats, nodes)


def bucket_kernel(
    count_ref, t_ref, node_ref, block_ref, pos_ref, weight_ref, out_ref, table, acc, carry
):
    step = pl.program_id(0)
    rb = node_ref.shape[1]

    @pl.when(step == 0)
    def _():
        acc[...] = jnp.zeros_like(acc)
        carry[...] = jnp.zeros_like(carry)
        table[...] = split_table(t_ref[...])

    node, pos, block = node_ref[...], pos_ref[...], block_ref[...]
    row = step * rb + iota((1, rb), 1)
    coef = jnp.where(row < count_ref[0], weight_ref[...], 0.0)
    bucket = to_bf((block & 7) * 16 + (block >> 3))

    owner = onehot(128, bucket)
    upper = jnp.where(iota((rb, rb), 0) <= iota((rb, rb), 1), 1.0, 0.0).astype(bf16)
    counts = jnp.dot(owner, upper, preferred_element_type=f32)
    before = carry[:, 0:1]
    rank = jnp.sum(owner.astype(f32) * (counts + before), axis=0, keepdims=True) - 1.0
    carry[...] = jnp.broadcast_to(before + counts[:, rb - 1 : rb], carry.shape)
    slot = onehot(256, rank.astype(bf16))

    x = pick(table[...], onehot(256, to_bf(node & 255)), node >> 8, 16)
    vals = split8(x * coef)
    hi = coef.astype(bf16).astype(f32)
    sub = iota((8, rb), 0)
    rest = jnp.zeros((8, rb), f32)
    highs = (pos >> 7).astype(f32), (node >> 8).astype(f32), hi
    lows = (pos & 127).astype(f32), (node & 255).astype(f32), coef - hi
    for i in range(3):
        rest = jnp.where(sub == i, jnp.broadcast_to(highs[i], (8, rb)), rest)
        rest = jnp.where(sub == i + 4, jnp.broadcast_to(lows[i], (8, rb)), rest)
    p16 = jnp.concatenate([vals.astype(bf16), rest.astype(bf16)], 0)
    b16 = jnp.broadcast_to(bucket, p16.shape)
    zero = jnp.zeros((), bf16)
    m2 = jnp.concatenate(
        [jnp.where(b16 == jnp.asarray(b, bf16), p16, zero) for b in range(128)], 0
    )
    acc[...] += lax.dot_general(m2, slot, NT, preferred_element_type=f32)

    @pl.when(step == pl.num_programs(0) - 1)
    def _():
        @pl.loop(0, 128)
        def _(b):
            at = pl.multiple_of(b * 16, 16)
            a = acc[pl.ds(at, 8), :]
            c = acc[pl.ds(at + 8, 8), :]
            s = iota(c.shape, 0)
            c = c * jnp.where(s == 0, 128.0, jnp.where(s == 1, 256.0, 1.0))
            out_ref[b] = jnp.where(s < 4, a + pltpu.roll(a, 4, axis=0), c + pltpu.roll(c, 4, axis=0))


def bucket_call(count, table, node, block, pos, weight):
    rows = node.shape[1]
    rb = 512
    row_spec = pl.BlockSpec((1, rb), lambda i: (0, i))
    return pl.pallas_call(
        bucket_kernel,
        grid=(rows // rb,),
        in_specs=[
            pl.BlockSpec(memory_space=pltpu.SMEM),
            pl.BlockSpec((128, 256), lambda i: (0, 0)),
            row_spec,
            row_spec,
            row_spec,
            row_spec,
        ],
        out_specs=pl.BlockSpec((128, 8, 256), lambda i: (0, 0, 0)),
        out_shape=jax.ShapeDtypeStruct((128, 8, 256), f32),
        scratch_shapes=[
            pltpu.VMEM((128, 512), bf16),
            pltpu.VMEM((2048, 256), f32),
            pltpu.VMEM((128, 128), f32),
        ],
        compiler_params=pltpu.CompilerParams(vmem_limit_bytes=VMEM_LIMIT),
        name="buckets",
    )(count, table, node, block, pos, weight)


def exchange_kernel(src, dst, send_sem, recv_sem, local_sem):
    count = 128
    wide = lax.axis_size("bem")
    me = lax.axis_index("fem") * wide + lax.axis_index("bem")
    barrier = pltpu.get_barrier_semaphore()

    @pl.loop(1, count)
    def _(k):
        peer = lax.rem(me + k, count)
        pl.semaphore_signal(
            barrier, inc=1, device_id=(peer // wide, lax.rem(peer, wide)), device_id_type=MESH
        )

    own = pltpu.make_async_copy(src.at[me], dst.at[me], local_sem)
    own.start()
    pl.semaphore_wait(barrier, count - 1)

    @pl.loop(1, count)
    def _(k):
        peer = lax.rem(me + k, count)
        pltpu.make_async_remote_copy(
            src_ref=src.at[peer],
            dst_ref=dst.at[me],
            send_sem=send_sem,
            recv_sem=recv_sem,
            device_id=(peer // wide, lax.rem(peer, wide)),
            device_id_type=MESH,
        ).start()

    own.wait()
    most = pl.ds(0, count - 1)
    pltpu.make_async_copy(src.at[most], src.at[most], send_sem).wait()
    pltpu.make_async_copy(dst.at[most], dst.at[most], recv_sem).wait()


def exchange_call(parts, collective_id, name):
    return pl.pallas_call(
        exchange_kernel,
        in_specs=[pl.BlockSpec(memory_space=pltpu.VMEM)],
        out_specs=pl.BlockSpec(memory_space=pltpu.VMEM),
        out_shape=jax.ShapeDtypeStruct(parts.shape, f32),
        scratch_shapes=[pltpu.SemaphoreType.DMA] * 3,
        compiler_params=pltpu.CompilerParams(
            collective_id=collective_id, has_side_effects=True, vmem_limit_bytes=VMEM_LIMIT
        ),
        name=name,
    )(parts)


def owner_kernel(got_ref, left_ref, near_ref, coupling_ref, near_out_ref, acc):
    step = pl.program_id(0)

    @pl.when(step == 0)
    def _():
        acc[...] = jnp.zeros_like(acc)

    tile = jnp.concatenate([got_ref[s] for s in range(got_ref.shape[0])], 1)
    vals = jnp.where(iota(tile.shape, 0) < 4, tile, pltpu.roll(tile, 4, axis=0))
    pos = tile[4:5].astype(i32)
    acc[...] += lax.dot_general(
        spread(split8(vals), pos >> 7, 5),
        onehot(128, to_bf(pos & 127)),
        NT,
        preferred_element_type=f32,
    )

    @pl.when(step == pl.num_programs(0) - 1)
    def _():
        parts = []
        for t in range(9):
            a = acc[8 * t : 8 * t + 8]
            part = split8(a + pltpu.roll(a, 4, axis=0)).astype(bf16)
            parts.append(part)
            n = jnp.dot(part, near_ref[t], preferred_element_type=f32)
            near_out_ref[:, 128 * t : 128 * t + 128] = (n + pltpu.roll(n, 4, axis=0))[0:4]
        c = lax.dot_general(
            jnp.concatenate(parts, 1), left_ref[...], NT, preferred_element_type=f32
        )
        coupling_ref[...] = (c + pltpu.roll(c, 4, axis=0))[0:4]


def owner_call(got, left, near):
    sb = 4
    return pl.pallas_call(
        owner_kernel,
        grid=(128 // sb,),
        in_specs=[
            pl.BlockSpec((sb, 8, 256), lambda i: (i, 0, 0)),
            pl.BlockSpec((512, 1152), lambda i: (0, 0)),
            pl.BlockSpec((9, 128, 128), lambda i: (0, 0, 0)),
        ],
        out_specs=[
            pl.BlockSpec((4, 512), lambda i: (0, 0)),
            pl.BlockSpec((4, 1152), lambda i: (0, 0)),
        ],
        out_shape=[jax.ShapeDtypeStruct((4, 512), f32), jax.ShapeDtypeStruct((4, 1152), f32)],
        scratch_shapes=[pltpu.VMEM((80, 128), f32)],
        compiler_params=pltpu.CompilerParams(vmem_limit_bytes=VMEM_LIMIT),
        name="owner",
    )(got, left, near)


def flux_kernel(
    part_ref, near_ref, right_ref, field_ref, out_ref, parts, shares, sums, sems, local_sem
):
    fems, bems = 8, 16
    f, b = lax.axis_index("fem"), lax.axis_index("bem")
    barrier = pltpu.get_barrier_semaphore()
    for k in range(1, fems):
        pl.semaphore_signal(
            barrier, inc=1, device_id=(lax.rem(f + k, fems), b), device_id_type=MESH
        )
    for k in range(1, bems):
        pl.semaphore_signal(
            barrier, inc=1, device_id=(f, lax.rem(b + k, bems)), device_id_type=MESH
        )
    pl.semaphore_wait(barrier, fems + bems - 2)

    for k in range(1, fems):
        pltpu.make_async_remote_copy(
            src_ref=part_ref,
            dst_ref=parts.at[f],
            send_sem=sems.at[0],
            recv_sem=sems.at[1],
            device_id=(lax.rem(f + k, fems), b),
            device_id_type=MESH,
        ).start()
    own = pltpu.make_async_copy(part_ref, parts.at[f], local_sem)
    own.start()
    own.wait()
    most = parts.at[pl.ds(0, fems - 1)]
    pltpu.make_async_copy(most, most, sems.at[0]).wait()
    pltpu.make_async_copy(most, most, sems.at[1]).wait()

    total = parts[0]
    for k in range(1, fems):
        total = total + parts[k]
    for half in range(2):
        c = total[:, 256 * half : 256 * half + 256]
        c = split8(jnp.concatenate([c, c], 0))
        stacked = jnp.concatenate([c] * 8, 0)
        shape = stacked.shape
        diag = jnp.where((iota(shape, 0) >> 3) == (iota(shape, 1) >> 5), stacked, 0.0).astype(bf16)
        far = jnp.dot(
            diag, right_ref[256 * half : 256 * half + 256], preferred_element_type=f32
        )
        for s in range(8):
            a = far[8 * s : 8 * s + 8]
            shares[8 * half + s] = (a + pltpu.roll(a, 4, axis=0))[0:4]
    shares[b] = shares[b] + near_ref[...]

    for k in range(1, bems):
        peer = lax.rem(b + k, bems)
        pltpu.make_async_remote_copy(
            src_ref=shares.at[peer],
            dst_ref=sums.at[b],
            send_sem=sems.at[2],
            recv_sem=sems.at[3],
            device_id=(f, peer),
            device_id_type=MESH,
        ).start()
    own = pltpu.make_async_copy(shares.at[b], sums.at[b], local_sem)
    own.start()
    own.wait()
    most = sums.at[pl.ds(0, bems - 1)]
    pltpu.make_async_copy(most, most, sems.at[2]).wait()
    pltpu.make_async_copy(most, most, sems.at[3]).wait()
    flux = field_ref[...]
    for k in range(bems):
        flux = flux + sums[k]
    out_ref[...] = flux


def flux_call(part, near, right, field):
    vmem = pl.BlockSpec(memory_space=pltpu.VMEM)
    return pl.pallas_call(
        flux_kernel,
        in_specs=[vmem] * 4,
        out_specs=vmem,
        out_shape=jax.ShapeDtypeStruct((4, 1152), f32),
        scratch_shapes=[
            pltpu.VMEM((8, 4, 512), f32),
            pltpu.VMEM((16, 4, 1152), f32),
            pltpu.VMEM((16, 4, 1152), f32),
            pltpu.SemaphoreType.DMA((4,)),
            pltpu.SemaphoreType.DMA,
        ],
        compiler_params=pltpu.CompilerParams(
            collective_id=1, has_side_effects=True, vmem_limit_bytes=VMEM_LIMIT
        ),
        name="flux",
    )(part, near, right, field)


def return_kernel(t_ref, got_ref, out_ref, table):
    @pl.when(first_step())
    def _():
        table[...] = split_table(t_ref[...])

    count = got_ref.shape[0]
    pos = jnp.concatenate([got_ref[s, 4:5] for s in range(count)], 1).astype(i32)
    x = pick(table[...], onehot(128, to_bf(pos & 127)), pos >> 7, 5)
    for s in range(count):
        out_ref[s] = x[0:4, 256 * s : 256 * s + 256]


def return_call(table, got):
    sb = 4
    return pl.pallas_call(
        return_kernel,
        grid=(128 // sb,),
        in_specs=[
            pl.BlockSpec((40, 128), lambda i: (0, 0)),
            pl.BlockSpec((sb, 8, 256), lambda i: (i, 0, 0)),
        ],
        out_specs=pl.BlockSpec((sb, 4, 256), lambda i: (i, 0, 0)),
        out_shape=jax.ShapeDtypeStruct((128, 4, 256), f32),
        scratch_shapes=[pltpu.VMEM((40, 256), bf16)],
        compiler_params=pltpu.CompilerParams(vmem_limit_bytes=VMEM_LIMIT),
        name="returns",
    )(table, got)


def nodes_kernel(stiff_ref, flux_ref, slots_ref, out_ref):
    @pl.when(first_step())
    def _():
        out_ref[...] = stiff_ref[...]

    count = flux_ref.shape[0]
    slots = jnp.concatenate([slots_ref[s] for s in range(count)], 1)
    x = jnp.concatenate([flux_ref[s] for s in range(count)], 1)
    coef = slots[6:7]
    node = slots[5:6].astype(i32)
    x = jnp.concatenate([x, x], 0) * coef
    out_ref[...] += lax.dot_general(
        spread(split8(x), node >> 8, 16),
        onehot(256, to_bf(node & 255)),
        NT,
        preferred_element_type=f32,
    )


def nodes_call(stiff, flux, slots):
    sb = 4
    return pl.pallas_call(
        nodes_kernel,
        grid=(128 // sb,),
        in_specs=[
            pl.BlockSpec((256, 256), lambda i: (0, 0)),
            pl.BlockSpec((sb, 4, 256), lambda i: (i, 0, 0)),
            pl.BlockSpec((sb, 8, 256), lambda i: (i, 0, 0)),
        ],
        out_specs=pl.BlockSpec((256, 256), lambda i: (0, 0)),
        out_shape=jax.ShapeDtypeStruct((256, 256), f32),
        compiler_params=pltpu.CompilerParams(vmem_limit_bytes=VMEM_LIMIT),
        name="nodes",
    )(stiff, flux, slots)


def tiles(x, width):
    return x.reshape(4, -1, width).transpose(1, 0, 2).reshape(-1, width)


def per_device(
    fem_field,
    elem_mats,
    elem_nodes,
    trace_count,
    trace_node,
    trace_block,
    trace_pos,
    trace_weight,
    near_tiles,
    left_basis,
    right_basis,
    bem_field,
):
    both = ("fem", "bem")
    size = lax.axis_size(both)
    ahead = [(i, i + 1) for i in range(size - 1)]
    back = [(i + 1, i) for i in range(size - 1)]
    low = lax.ppermute(fem_field[:, -REACH:], both, ahead)
    high = lax.ppermute(fem_field[:, :REACH], both, back)
    own_table = tiles(fem_field, 256)
    table = jnp.concatenate([tiles(low, 256), own_table, tiles(high, 256)], 0)

    slots = bucket_call(
        trace_count,
        own_table,
        trace_node.reshape(1, -1),
        trace_block.reshape(1, -1),
        trace_pos.reshape(1, -1),
        trace_weight.reshape(1, -1),
    )
    got = exchange_call(slots, 0, "rows_out")
    stiff = elem_call(table, elem_mats.reshape(16, -1), elem_nodes)
    part, near = owner_call(got, left_basis.reshape(512, 1152), near_tiles[0])
    flux = flux_call(part, near, right_basis.reshape(512, 1152), bem_field[0])
    flux_table = jnp.concatenate([tiles(flux, 128), jnp.zeros((4, 128), f32)], 0)
    returned = exchange_call(return_call(flux_table, got), 2, "flux_back")
    out = nodes_call(stiff, returned, slots)
    out = out.reshape(32, 2, 4, 256).sum(1).transpose(1, 0, 2).reshape(4, -1)
    return out, flux[None]


def solution(mesh):
    placed = (
        P(None, ("fem", "bem")),
        P(None, None, ("fem", "bem")),
        P(None, ("fem", "bem")),
        P(("fem", "bem")),
        P(("fem", "bem")),
        P(("fem", "bem"), None),
        P(("fem", "bem")),
        P(("fem", "bem")),
        P("bem", "fem", None, None),
        P("bem", None, None, "fem"),
        P("bem", None, None, "fem"),
        P("bem", None, "fem"),
    )
    return jax.shard_map(
        per_device,
        mesh=mesh,
        in_specs=placed,
        out_specs=(P(None, ("fem", "bem")), P("bem", None, "fem")),
        check_vma=False,
    )
```

```python
import functools

import jax
import jax.numpy as jnp
from jax import lax
from jax.experimental import pallas as pl
from jax.experimental.pallas import tpu as pltpu
from jax.sharding import PartitionSpec as P

ELEM_BLOCK = 2048
SHARE_ROWS = (0, 9)
SHARE_COUPLING = (9, 1)
SHARE_FLUX = (10, 2)
SHARE_BACK = (12, 4)
bf16 = jnp.bfloat16
f32 = jnp.float32
i32 = jnp.int32
MESH = pl.DeviceIdType.MESH
NT = (((1,), (1,)), ((), ()))
VMEM_LIMIT = 48 << 20


def iota(shape, dim):
    return lax.broadcasted_iota(i32, shape, dim)


def to_bf(x):
    return x.astype(f32).astype(bf16)


def onehot(rows, index):
    shape = (rows, index.shape[1])
    return jnp.where(
        to_bf(iota(shape, 0)) == jnp.broadcast_to(index, shape),
        jnp.ones((), bf16),
        jnp.zeros((), bf16),
    )


def split8(x):
    hi = x.astype(bf16).astype(f32)
    return jnp.where(iota(x.shape, 0) < 4, hi, x - hi)


def split_table(t):
    hi = t.astype(bf16)
    return jnp.concatenate([hi, (t - hi.astype(f32)).astype(bf16)], 1)


def pick(table, hot, q, groups):
    r = jnp.dot(table, jnp.concatenate([hot, hot], 0), preferred_element_type=f32)
    shape = (8, hot.shape[1])
    qh = jnp.broadcast_to(q, shape) - jnp.where(iota(shape, 0) >= 4, 1, 0)
    acc = jnp.where(qh == 0, r[0:8], 0.0)
    for j in range(1, groups):
        acc = jnp.where(qh == 2 * j, r[8 * j : 8 * j + 8], acc)
    return acc + pltpu.roll(acc, 4, axis=0)


def spread(part, q, groups):
    part = part.astype(bf16)
    p16 = jnp.concatenate([part, part], 0)
    qv = to_bf(jnp.broadcast_to(q, p16.shape) - jnp.where(iota(p16.shape, 0) >= 8, 1, 0))
    zero = jnp.zeros((), bf16)
    return jnp.concatenate(
        [jnp.where(qv == jnp.asarray(2 * j, bf16), p16, zero) for j in range(groups)], 0
    )


def elem_blocks(table, mats_ref, nodes_ref, out_ref, first, blocks):
    @pl.loop(first, first + blocks)
    def _(i):
        at = pl.ds(pl.multiple_of(i * ELEM_BLOCK, ELEM_BLOCK), ELEM_BLOCK)
        nodes = nodes_ref[:, at]
        hots, xs = [], []
        for a in range(4):
            n = nodes[a : a + 1]
            hot = onehot(256, to_bf(n & 255))
            hots.append(hot)
            xs.append(pick(table[...], hot, n >> 8, 18))
        total = None
        for b in range(4):
            c = mats_ref[0, pl.ds(b, 1), at] * xs[0]
            for a in range(1, 4):
                c = c + mats_ref[a, pl.ds(b, 1), at] * xs[a]
            d = lax.dot_general(
                spread(split8(c), (nodes[b : b + 1] >> 8) - 2, 16),
                hots[b],
                NT,
                preferred_element_type=f32,
            )
            total = d if total is None else total + d
        out_ref[...] += total


def bucket_kernel(count_ref, node_ref, block_ref, pos_ref, weight_ref, out_ref, acc, carry):
    step = pl.program_id(0)
    rb = node_ref.shape[1]

    @pl.when(step == 0)
    def _():
        acc[...] = jnp.zeros_like(acc)
        carry[...] = jnp.zeros_like(carry)

    node, pos, block = node_ref[...], pos_ref[...], block_ref[...]
    row = step * rb + iota((1, rb), 1)
    coef = jnp.where(row < count_ref[0], weight_ref[...], 0.0)
    bucket = (block & 7) * 16 + (block >> 3)

    owner = onehot(128, to_bf(bucket))
    upper = jnp.where(iota((256, 256), 0) <= iota((256, 256), 1), 1.0, 0.0).astype(bf16)
    before = carry[:, 0:1]
    ranks = []
    for at in range(0, rb, 256):
        hot = owner[:, at : at + 256]
        counts = jnp.dot(hot, upper, preferred_element_type=f32) + before
        ranks.append(jnp.sum(hot.astype(f32) * counts, axis=0, keepdims=True) - 1.0)
        before = counts[:, 255:256]
    carry[...] = jnp.broadcast_to(before, carry.shape)
    slot = onehot(256, jnp.concatenate(ranks, 1).astype(bf16))

    hi = coef.astype(bf16).astype(f32)
    sub = iota((8, rb), 0)
    part = jnp.zeros((8, rb), f32)
    highs = (pos >> 7).astype(f32), (node >> 8).astype(f32), hi
    lows = (pos & 127).astype(f32), (node & 255).astype(f32), coef - hi
    for i in range(3):
        part = jnp.where(sub == i, jnp.broadcast_to(highs[i], (8, rb)), part)
        part = jnp.where(sub == i + 4, jnp.broadcast_to(lows[i], (8, rb)), part)
    acc[...] += lax.dot_general(spread(part, bucket, 64), slot, NT, preferred_element_type=f32)

    @pl.when(step == pl.num_programs(0) - 1)
    def _():
        @pl.loop(0, 128)
        def _(b):
            c = acc[pl.ds(pl.multiple_of(b * 8, 8), 8), :]
            s = iota(c.shape, 0)
            c = c * jnp.where(s == 0, 128.0, jnp.where(s == 1, 256.0, 1.0))
            out_ref[b] = c + pltpu.roll(c, 4, axis=0)


def bucket_call(count, node, block, pos, weight):
    rows = node.shape[1]
    rb = 1024
    row_spec = pl.BlockSpec((1, rb), lambda i: (0, i))
    return pl.pallas_call(
        bucket_kernel,
        grid=(rows // rb,),
        in_specs=[pl.BlockSpec(memory_space=pltpu.SMEM)] + [row_spec] * 4,
        out_specs=pl.BlockSpec((128, 8, 256), lambda i: (0, 0, 0)),
        out_shape=jax.ShapeDtypeStruct((128, 8, 256), f32),
        scratch_shapes=[pltpu.VMEM((1024, 256), f32), pltpu.VMEM((128, 128), f32)],
        compiler_params=pltpu.CompilerParams(vmem_limit_bytes=VMEM_LIMIT),
        name="buckets",
    )(count, node, block, pos, weight)


DEVICES = 128


def place(index):
    wide = lax.axis_size("bem")
    return (index // wide, lax.rem(index, wide))


def greet_all(me):
    barrier = pltpu.get_barrier_semaphore()

    @pl.loop(1, DEVICES)
    def _(k):
        pl.semaphore_signal(
            barrier, inc=1, device_id=place(lax.rem(me + k, DEVICES)), device_id_type=MESH
        )


def await_all():
    pl.semaphore_wait(pltpu.get_barrier_semaphore(), DEVICES - 1)


def wait_bytes(ref, sem):
    pltpu.make_async_copy(ref, ref, sem).wait()


def send_chunks(me, send, got, sems, fill):
    group = 8

    def chunk(i, last):
        peers = [lax.rem(me + i * group + j + 1, DEVICES) for j in range(group)]
        fill(peers)
        for peer in peers[: group - 1] if last else peers:
            pltpu.make_async_remote_copy(
                src_ref=send.at[peer],
                dst_ref=got.at[me],
                send_sem=sems.at[0],
                recv_sem=sems.at[1],
                device_id=place(peer),
                device_id_type=MESH,
            ).start()

    @pl.loop(0, DEVICES // group - 1)
    def _(i):
        chunk(i, False)

    chunk(DEVICES // group - 1, True)
    got[me] = send[me]


def wait_chunks(send, got, sems):
    most = pl.ds(0, DEVICES - 1)
    wait_bytes(send.at[most], sems.at[0])
    wait_bytes(got.at[most], sems.at[1])


def device_index():
    return lax.axis_index("fem") * lax.axis_size("bem") + lax.axis_index("bem")


def rows_kernel(
    slots_ref, field_ref, mats_ref, nodes_ref, got, stiff_ref, table, own, halo, send, sems, halo_sems
):
    me = device_index()
    greet_all(me)
    own[...] = split_table(field_ref[...])
    stiff_ref[...] = jnp.zeros_like(stiff_ref)
    await_all()

    right, left = lax.rem(me + 1, DEVICES), lax.rem(me + DEVICES - 1, DEVICES)
    up = pltpu.make_async_remote_copy(
        src_ref=field_ref.at[pl.ds(120, 8)],
        dst_ref=halo.at[0],
        send_sem=halo_sems.at[0],
        recv_sem=halo_sems.at[1],
        device_id=place(right),
        device_id_type=MESH,
    )
    down = pltpu.make_async_remote_copy(
        src_ref=field_ref.at[pl.ds(0, 8)],
        dst_ref=halo.at[1],
        send_sem=halo_sems.at[2],
        recv_sem=halo_sems.at[3],
        device_id=place(left),
        device_id_type=MESH,
    )
    up.start()
    down.start()

    def fill(peers):
        tiles = [slots_ref[p] for p in peers]
        node = jnp.concatenate([t[1:2] for t in tiles], 1).astype(i32)
        coef = jnp.concatenate([t[2:3] for t in tiles], 1)
        x = pick(own[...], onehot(256, to_bf(node & 255)), node >> 8, 16) * coef
        for j, p in enumerate(peers):
            send[p, 0:4] = x[0:4, 256 * j : 256 * j + 256]
            send[p, 4:5] = tiles[j][0:1]

    send_chunks(me, send, got, sems, fill)

    up.wait()
    down.wait()
    low = jnp.where(me == 0, 0.0, halo[0])
    high = jnp.where(me == DEVICES - 1, 0.0, halo[1])
    table[0:8] = split_table(low)
    table[8:136] = own[...]
    table[136:144] = split_table(high)
    elem_blocks(table, mats_ref, nodes_ref, stiff_ref, *SHARE_ROWS)
    wait_chunks(send, got, sems)


def rows_call(slots, field, mats, nodes):
    vmem = pl.BlockSpec(memory_space=pltpu.VMEM)
    return pl.pallas_call(
        rows_kernel,
        in_specs=[vmem] * 4,
        out_specs=[vmem] * 3,
        out_shape=[
            jax.ShapeDtypeStruct((DEVICES, 5, 256), f32),
            jax.ShapeDtypeStruct((256, 256), f32),
            jax.ShapeDtypeStruct((144, 512), bf16),
        ],
        scratch_shapes=[
            pltpu.VMEM((128, 512), bf16),
            pltpu.VMEM((2, 8, 256), f32),
            pltpu.VMEM((DEVICES, 5, 256), f32),
            pltpu.SemaphoreType.DMA((2,)),
            pltpu.SemaphoreType.DMA((4,)),
        ],
        compiler_params=pltpu.CompilerParams(
            collective_id=0, has_side_effects=True, vmem_limit_bytes=VMEM_LIMIT
        ),
        name="rows_out",
    )(slots, field, mats, nodes)


def flux_kernel(
    got_ref,
    left_ref,
    near_ref,
    right_ref,
    field_ref,
    table,
    mats_ref,
    nodes_ref,
    out_ref,
    stiff_ref,
    acc,
    part_ref,
    near_out,
    parts,
    shares,
    sums,
    sems,
):
    fems, bems = 8, 16
    f, b = lax.axis_index("fem"), lax.axis_index("bem")
    barrier = pltpu.get_barrier_semaphore()
    for k in range(1, fems):
        pl.semaphore_signal(
            barrier, inc=1, device_id=(lax.rem(f + k, fems), b), device_id_type=MESH
        )
    for k in range(1, bems):
        pl.semaphore_signal(
            barrier, inc=1, device_id=(f, lax.rem(b + k, bems)), device_id_type=MESH
        )
    acc[...] = jnp.zeros_like(acc)
    stiff_ref[...] = jnp.zeros_like(stiff_ref)
    group = 16

    @pl.loop(0, DEVICES // group)
    def _(i):
        tiles = [got_ref[i * group + j] for j in range(group)]
        vals = jnp.concatenate([t[0:4] for t in tiles], 1)
        pos = jnp.concatenate([t[4:5] for t in tiles], 1).astype(i32)
        acc[...] += lax.dot_general(
            spread(split8(jnp.concatenate([vals, vals], 0)), pos >> 7, 5),
            onehot(128, to_bf(pos & 127)),
            NT,
            preferred_element_type=f32,
        )

    pieces = []
    for t in range(9):
        a = acc[8 * t : 8 * t + 8]
        piece = split8(a + pltpu.roll(a, 4, axis=0)).astype(bf16)
        pieces.append(piece)
        n = jnp.dot(piece, near_ref[t], preferred_element_type=f32)
        near_out[:, 128 * t : 128 * t + 128] = (n + pltpu.roll(n, 4, axis=0))[0:4]
    c = lax.dot_general(jnp.concatenate(pieces, 1), left_ref[...], NT, preferred_element_type=f32)
    part_ref[...] = (c + pltpu.roll(c, 4, axis=0))[0:4]

    pl.semaphore_wait(barrier, fems + bems - 2)
    for k in range(1, fems):
        pltpu.make_async_remote_copy(
            src_ref=part_ref,
            dst_ref=parts.at[f],
            send_sem=sems.at[0],
            recv_sem=sems.at[1],
            device_id=(lax.rem(f + k, fems), b),
            device_id_type=MESH,
        ).start()
    parts[f] = part_ref[...]
    elem_blocks(table, mats_ref, nodes_ref, stiff_ref, *SHARE_COUPLING)
    most = parts.at[pl.ds(0, fems - 1)]
    wait_bytes(most, sems.at[0])
    wait_bytes(most, sems.at[1])

    total = parts[0]
    for k in range(1, fems):
        total = total + parts[k]
    for half in range(2):
        c = total[:, 256 * half : 256 * half + 256]
        c = split8(jnp.concatenate([c, c], 0))
        stacked = jnp.concatenate([c] * 8, 0)
        shape = stacked.shape
        diag = jnp.where((iota(shape, 0) >> 3) == (iota(shape, 1) >> 5), stacked, 0.0).astype(bf16)
        far = jnp.dot(
            diag, right_ref[256 * half : 256 * half + 256], preferred_element_type=f32
        )
        for s in range(8):
            a = far[8 * s : 8 * s + 8]
            shares[8 * half + s] = (a + pltpu.roll(a, 4, axis=0))[0:4]
    shares[b] = shares[b] + near_out[...]

    for k in range(1, bems):
        peer = lax.rem(b + k, bems)
        pltpu.make_async_remote_copy(
            src_ref=shares.at[peer],
            dst_ref=sums.at[b],
            send_sem=sems.at[2],
            recv_sem=sems.at[3],
            device_id=(f, peer),
            device_id_type=MESH,
        ).start()
    sums[b] = shares[b]
    elem_blocks(table, mats_ref, nodes_ref, stiff_ref, *SHARE_FLUX)
    most = sums.at[pl.ds(0, bems - 1)]
    wait_bytes(most, sems.at[2])
    wait_bytes(most, sems.at[3])
    flux = field_ref[...]
    for k in range(bems):
        flux = flux + sums[k]
    out_ref[...] = flux


def flux_call(*args):
    vmem = pl.BlockSpec(memory_space=pltpu.VMEM)
    return pl.pallas_call(
        flux_kernel,
        in_specs=[vmem] * 8,
        out_specs=[vmem] * 2,
        out_shape=[jax.ShapeDtypeStruct((4, 1152), f32), jax.ShapeDtypeStruct((256, 256), f32)],
        scratch_shapes=[
            pltpu.VMEM((80, 128), f32),
            pltpu.VMEM((4, 512), f32),
            pltpu.VMEM((4, 1152), f32),
            pltpu.VMEM((8, 4, 512), f32),
            pltpu.VMEM((16, 4, 1152), f32),
            pltpu.VMEM((16, 4, 1152), f32),
            pltpu.SemaphoreType.DMA((4,)),
        ],
        compiler_params=pltpu.CompilerParams(
            collective_id=1, has_side_effects=True, vmem_limit_bytes=VMEM_LIMIT
        ),
        name="flux",
    )(*args)


def back_kernel(
    flux_ref, rows_ref, table, mats_ref, nodes_ref, got, stiff_ref, flux_f32, flux_table, send, sems
):
    me = device_index()
    greet_all(me)
    flux_f32[...] = jnp.zeros_like(flux_f32)
    for t in range(9):
        flux_f32[4 * t : 4 * t + 4] = flux_ref[:, 128 * t : 128 * t + 128]
    flux_table[...] = split_table(flux_f32[...])
    stiff_ref[...] = jnp.zeros_like(stiff_ref)
    await_all()

    def fill(peers):
        pos = jnp.concatenate([rows_ref[p, 4:5] for p in peers], 1).astype(i32)
        x = pick(flux_table[...], onehot(128, to_bf(pos & 127)), pos >> 7, 5)
        for j, p in enumerate(peers):
            send[p] = x[0:4, 256 * j : 256 * j + 256]

    send_chunks(me, send, got, sems, fill)
    elem_blocks(table, mats_ref, nodes_ref, stiff_ref, *SHARE_BACK)
    wait_chunks(send, got, sems)


def back_call(*args):
    vmem = pl.BlockSpec(memory_space=pltpu.VMEM)
    return pl.pallas_call(
        back_kernel,
        in_specs=[vmem] * 5,
        out_specs=[vmem] * 2,
        out_shape=[
            jax.ShapeDtypeStruct((DEVICES, 4, 256), f32),
            jax.ShapeDtypeStruct((256, 256), f32),
        ],
        scratch_shapes=[
            pltpu.VMEM((40, 128), f32),
            pltpu.VMEM((40, 256), bf16),
            pltpu.VMEM((DEVICES, 4, 256), f32),
            pltpu.SemaphoreType.DMA((2,)),
        ],
        compiler_params=pltpu.CompilerParams(
            collective_id=2, has_side_effects=True, vmem_limit_bytes=VMEM_LIMIT
        ),
        name="flux_back",
    )(*args)


def nodes_kernel(stiff_a, stiff_b, stiff_c, flux_ref, slots_ref, out_ref, acc):
    step = pl.program_id(0)

    @pl.when(step == 0)
    def _():
        acc[...] = stiff_a[...] + stiff_b[...] + stiff_c[...]

    count = flux_ref.shape[0]
    node = jnp.concatenate([slots_ref[s, 1:2] for s in range(count)], 1).astype(i32)
    coef = jnp.concatenate([slots_ref[s, 2:3] for s in range(count)], 1)
    x = jnp.concatenate([flux_ref[s] for s in range(count)], 1)
    x = jnp.concatenate([x, x], 0) * coef
    acc[...] += lax.dot_general(
        spread(split8(x), node >> 8, 16),
        onehot(256, to_bf(node & 255)),
        NT,
        preferred_element_type=f32,
    )

    @pl.when(step == pl.num_programs(0) - 1)
    def _():
        for q in range(32):
            a = acc[8 * q : 8 * q + 8]
            out_ref[:, 256 * q : 256 * q + 256] = (a + pltpu.roll(a, 4, axis=0))[0:4]


def nodes_call(stiffs, flux, slots):
    sb = 16
    whole = pl.BlockSpec((256, 256), lambda i: (0, 0))
    return pl.pallas_call(
        nodes_kernel,
        grid=(DEVICES // sb,),
        in_specs=[whole] * 3
        + [
            pl.BlockSpec((sb, 4, 256), lambda i: (i, 0, 0)),
            pl.BlockSpec((sb, 8, 256), lambda i: (i, 0, 0)),
        ],
        out_specs=pl.BlockSpec((4, 8192), lambda i: (0, 0)),
        out_shape=jax.ShapeDtypeStruct((4, 8192), f32),
        scratch_shapes=[pltpu.VMEM((256, 256), f32)],
        compiler_params=pltpu.CompilerParams(vmem_limit_bytes=VMEM_LIMIT),
        name="nodes",
    )(*stiffs, flux, slots)


def tiles(x, width):
    return x.reshape(4, -1, width).transpose(1, 0, 2).reshape(-1, width)


def per_device(
    fem_field,
    elem_mats,
    elem_nodes,
    trace_count,
    trace_node,
    trace_block,
    trace_pos,
    trace_weight,
    near_tiles,
    left_basis,
    right_basis,
    bem_field,
):
    slots = bucket_call(
        trace_count,
        trace_node.reshape(1, -1),
        trace_block.reshape(1, -1),
        trace_pos.reshape(1, -1),
        trace_weight.reshape(1, -1),
    )
    got, stiff_a, table = rows_call(slots, tiles(fem_field, 256), elem_mats, elem_nodes)
    flux, stiff_b = flux_call(
        got,
        left_basis.reshape(512, 1152),
        near_tiles[0],
        right_basis.reshape(512, 1152),
        bem_field[0],
        table,
        elem_mats,
        elem_nodes,
    )
    returned, stiff_c = back_call(flux, got, table, elem_mats, elem_nodes)
    out = nodes_call((stiff_a, stiff_b, stiff_c), returned, slots)
    return out, flux[None]


def solution(mesh):
    placed = (
        P(None, ("fem", "bem")),
        P(None, None, ("fem", "bem")),
        P(None, ("fem", "bem")),
        P(("fem", "bem")),
        P(("fem", "bem")),
        P(("fem", "bem"), None),
        P(("fem", "bem")),
        P(("fem", "bem")),
        P("bem", "fem", None, None),
        P("bem", None, None, "fem"),
        P("bem", None, None, "fem"),
        P("bem", None, "fem"),
    )
    return jax.shard_map(
        per_device,
        mesh=mesh,
        in_specs=placed,
        out_specs=(P(None, ("fem", "bem")), P("bem", None, "fem")),
        check_vma=False,
    )
```

```python
import functools

import jax
import jax.numpy as jnp
from jax import lax
from jax.experimental import pallas as pl
from jax.experimental.pallas import tpu as pltpu
from jax.sharding import PartitionSpec as P

ELEM_BLOCK = 2048
ROW_BLOCK = 2048
SHARE_ROWS = (0, 6)
SHARE_COUPLING = (6, 2)
SHARE_FLUX = (8, 3)
SHARE_BACK = (11, 5)
bf16 = jnp.bfloat16
f32 = jnp.float32
i32 = jnp.int32
MESH = pl.DeviceIdType.MESH
NT = (((1,), (1,)), ((), ()))
VMEM_LIMIT = 63 << 20


def iota(shape, dim):
    return lax.broadcasted_iota(i32, shape, dim)


def to_bf(x):
    return x.astype(f32).astype(bf16)


def onehot(rows, index):
    shape = (rows, index.shape[1])
    return jnp.where(
        to_bf(iota(shape, 0)) == jnp.broadcast_to(index, shape),
        jnp.ones((), bf16),
        jnp.zeros((), bf16),
    )


def split8(x):
    hi = x.astype(bf16).astype(f32)
    return jnp.where(iota(x.shape, 0) < 4, hi, x - hi)


def split_table(t):
    hi = t.astype(bf16)
    return jnp.concatenate([hi, (t - hi.astype(f32)).astype(bf16)], 1)


def pick(table, hot, q, groups):
    r = jnp.dot(table, jnp.concatenate([hot, hot], 0), preferred_element_type=f32)
    shape = (8, hot.shape[1])
    qh = jnp.broadcast_to(q, shape) - jnp.where(iota(shape, 0) >= 4, 1, 0)
    acc = jnp.where(qh == 0, r[0:8], 0.0)
    for j in range(1, groups):
        acc = jnp.where(qh == 2 * j, r[8 * j : 8 * j + 8], acc)
    return acc + pltpu.roll(acc, 4, axis=0)


def spread(part, q, groups):
    part = part.astype(bf16)
    p16 = jnp.concatenate([part, part], 0)
    qv = to_bf(jnp.broadcast_to(q, p16.shape) - jnp.where(iota(p16.shape, 0) >= 8, 1, 0))
    zero = jnp.zeros((), bf16)
    return jnp.concatenate(
        [jnp.where(qv == jnp.asarray(2 * j, bf16), p16, zero) for j in range(groups)], 0
    )


def elem_blocks(table, mats_ref, nodes_ref, out_ref, first, blocks):
    @pl.loop(first, first + blocks)
    def _(i):
        at = pl.ds(pl.multiple_of(i * ELEM_BLOCK, ELEM_BLOCK), ELEM_BLOCK)
        nodes = nodes_ref[:, at]
        hots, xs = [], []
        for a in range(4):
            n = nodes[a : a + 1]
            hot = onehot(256, to_bf(n & 255))
            hots.append(hot)
            xs.append(pick(table[...], hot, n >> 8, 18))
        total = None
        for b in range(4):
            c = mats_ref[0, pl.ds(b, 1), at] * xs[0]
            for a in range(1, 4):
                c = c + mats_ref[a, pl.ds(b, 1), at] * xs[a]
            d = lax.dot_general(
                spread(split8(c), (nodes[b : b + 1] >> 8) - 2, 16),
                hots[b],
                NT,
                preferred_element_type=f32,
            )
            total = d if total is None else total + d
        out_ref[...] += total


def bucket_rows(count_ref, node_ref, block_ref, pos_ref, weight_ref, out_ref, acc):
    rb = ROW_BLOCK
    acc[...] = jnp.zeros_like(acc)

    def step(i, before):
        at = pl.ds(pl.multiple_of(i * rb, rb), rb)
        node, pos, block = node_ref[:, at], pos_ref[:, at], block_ref[:, at]
        row = i * rb + iota((1, rb), 1)
        coef = jnp.where(row < count_ref[0], weight_ref[:, at], 0.0)
        bucket = (block & 7) * 16 + (block >> 3)

        owner = onehot(128, to_bf(bucket))
        upper = jnp.where(iota((256, 256), 0) <= iota((256, 256), 1), 1.0, 0.0).astype(bf16)
        ranks = []
        for k in range(0, rb, 256):
            hot = owner[:, k : k + 256]
            counts = jnp.dot(hot, upper, preferred_element_type=f32) + before
            ranks.append(jnp.sum(hot.astype(f32) * counts, axis=0, keepdims=True) - 1.0)
            before = counts[:, 255:256]
        slot = onehot(256, jnp.concatenate(ranks, 1).astype(bf16))

        hi = coef.astype(bf16).astype(f32)
        sub = iota((8, rb), 0)
        part = jnp.zeros((8, rb), f32)
        highs = (pos >> 7).astype(f32), (node >> 8).astype(f32), hi
        lows = (pos & 127).astype(f32), (node & 255).astype(f32), coef - hi
        for k in range(3):
            part = jnp.where(sub == k, jnp.broadcast_to(highs[k], (8, rb)), part)
            part = jnp.where(sub == k + 4, jnp.broadcast_to(lows[k], (8, rb)), part)
        acc[...] += lax.dot_general(
            spread(part, bucket, 64), slot, NT, preferred_element_type=f32
        )
        return before

    lax.fori_loop(0, node_ref.shape[1] // rb, step, jnp.zeros((128, 1), f32))

    @pl.loop(0, 128)
    def _(b):
        c = acc[pl.ds(pl.multiple_of(b * 8, 8), 8), :]
        s = iota(c.shape, 0)
        c = c * jnp.where(s == 0, 128.0, jnp.where(s == 1, 256.0, 1.0))
        out_ref[b] = c + pltpu.roll(c, 4, axis=0)


DEVICES = 128


def place(index):
    wide = lax.axis_size("bem")
    return (index // wide, lax.rem(index, wide))


def greet_all(me):
    barrier = pltpu.get_barrier_semaphore()

    @pl.loop(1, DEVICES)
    def _(k):
        pl.semaphore_signal(
            barrier, inc=1, device_id=place(lax.rem(me + k, DEVICES)), device_id_type=MESH
        )


def await_all():
    pl.semaphore_wait(pltpu.get_barrier_semaphore(), DEVICES - 1)


def remote(src, dst, sems, at, device):
    return pltpu.make_async_remote_copy(
        src_ref=src,
        dst_ref=dst,
        send_sem=sems.at[at],
        recv_sem=sems.at[at + 1],
        device_id=device,
        device_id_type=MESH,
    )


def wait_bytes(ref, sem):
    pltpu.make_async_copy(ref, ref, sem).wait()


def send_chunks(me, send, got, sems, at, fill):
    group = 8

    def chunk(i, last):
        peers = [lax.rem(me + i * group + j + 1, DEVICES) for j in range(group)]
        fill(peers)
        for peer in peers[: group - 1] if last else peers:
            remote(send.at[peer], got.at[me], sems, at, place(peer)).start()

    @pl.loop(0, DEVICES // group - 1)
    def _(i):
        chunk(i, False)

    chunk(DEVICES // group - 1, True)
    got[me] = send[me]


def wait_copies(ref, count, sems, at):
    most = ref.at[pl.ds(0, count - 1)]
    wait_bytes(most, sems.at[at])
    wait_bytes(most, sems.at[at + 1])


def sum_rows(got, left, near, acc, near_out, part_ref):
    acc[...] = jnp.zeros_like(acc)
    group = 16

    @pl.loop(0, DEVICES // group)
    def _(i):
        tiles = [got[i * group + j] for j in range(group)]
        vals = jnp.concatenate([t[0:4] for t in tiles], 1)
        pos = jnp.concatenate([t[4:5] for t in tiles], 1).astype(i32)
        acc[...] += lax.dot_general(
            spread(split8(jnp.concatenate([vals, vals], 0)), pos >> 7, 5),
            onehot(128, to_bf(pos & 127)),
            NT,
            preferred_element_type=f32,
        )

    pieces = []
    for t in range(9):
        a = acc[8 * t : 8 * t + 8]
        piece = split8(a + pltpu.roll(a, 4, axis=0)).astype(bf16)
        pieces.append(piece)
        n = jnp.dot(piece, near[t], preferred_element_type=f32)
        near_out[:, 128 * t : 128 * t + 128] = (n + pltpu.roll(n, 4, axis=0))[0:4]
    c = lax.dot_general(jnp.concatenate(pieces, 1), left[...], NT, preferred_element_type=f32)
    part_ref[...] = (c + pltpu.roll(c, 4, axis=0))[0:4]


def far_field(parts, right, shares):
    total = parts[0]
    for k in range(1, parts.shape[0]):
        total = total + parts[k]
    for half in range(2):
        c = total[:, 256 * half : 256 * half + 256]
        c = split8(jnp.concatenate([c, c], 0))
        stacked = jnp.concatenate([c] * 8, 0)
        shape = stacked.shape
        diag = jnp.where((iota(shape, 0) >> 3) == (iota(shape, 1) >> 5), stacked, 0.0).astype(bf16)
        far = jnp.dot(diag, right[256 * half : 256 * half + 256], preferred_element_type=f32)
        for s in range(8):
            a = far[8 * s : 8 * s + 8]
            shares[8 * half + s] = (a + pltpu.roll(a, 4, axis=0))[0:4]


def add_returned(got, slots, acc):
    group = 16

    @pl.loop(0, DEVICES // group)
    def _(i):
        at = [i * group + j for j in range(group)]
        node = jnp.concatenate([slots[s, 1:2] for s in at], 1).astype(i32)
        coef = jnp.concatenate([slots[s, 2:3] for s in at], 1)
        x = jnp.concatenate([got[s] for s in at], 1)
        x = jnp.concatenate([x, x], 0) * coef
        acc[...] += lax.dot_general(
            spread(split8(x), node >> 8, 16),
            onehot(256, to_bf(node & 255)),
            NT,
            preferred_element_type=f32,
        )


def whole_kernel(
    count_ref,
    field_hbm,
    node_hbm,
    block_hbm,
    pos_hbm,
    weight_hbm,
    bem_hbm,
    mats_hbm,
    nodes_hbm,
    left_hbm,
    near_hbm,
    right_hbm,
    fem_out,
    flux_out,
    field,
    node_ref,
    block_ref,
    pos_ref,
    weight_ref,
    bem_ref,
    field_ref,
    mats,
    nodes,
    left,
    near,
    right,
    bucket_acc,
    slots,
    table,
    own,
    halo,
    send,
    got,
    row_acc,
    part_ref,
    near_out,
    parts,
    shares,
    sums,
    flux_f32,
    flux_table,
    send_back,
    got_back,
    stiff,
    sems,
    local_sems,
):
    fems, bems = lax.axis_size("fem"), lax.axis_size("bem")
    f, b = lax.axis_index("fem"), lax.axis_index("bem")
    me = f * bems + b
    pairs = [
        (block_hbm, block_ref),
        (node_hbm, node_ref),
        (pos_hbm, pos_ref),
        (weight_hbm, weight_ref),
        (field_hbm, field),
        (nodes_hbm, nodes),
        (mats_hbm, mats),
        (left_hbm, left),
        (near_hbm, near),
        (right_hbm, right),
        (bem_hbm, bem_ref),
    ]
    loads = [
        pltpu.make_async_copy(src, dst, local_sems.at[k]) for k, (src, dst) in enumerate(pairs)
    ]
    for load in loads:
        load.start()
    greet_all(me)
    stiff[...] = jnp.zeros_like(stiff)
    for load in loads[:5]:
        load.wait()
    for q in range(32):
        field_ref[4 * q : 4 * q + 4] = field[:, 256 * q : 256 * q + 256]
    own[...] = split_table(field_ref[...])
    bucket_rows(count_ref, node_ref, block_ref, pos_ref, weight_ref, slots, bucket_acc)

    await_all()
    up = remote(
        field_ref.at[pl.ds(120, 8)], halo.at[0], sems, 0, place(lax.rem(me + 1, DEVICES))
    )
    down = remote(
        field_ref.at[pl.ds(0, 8)], halo.at[1], sems, 2, place(lax.rem(me + DEVICES - 1, DEVICES))
    )
    up.start()
    down.start()

    def fill_rows(peers):
        parts8 = [slots[p] for p in peers]
        node = jnp.concatenate([t[1:2] for t in parts8], 1).astype(i32)
        coef = jnp.concatenate([t[2:3] for t in parts8], 1)
        x = pick(own[...], onehot(256, to_bf(node & 255)), node >> 8, 16) * coef
        for j, p in enumerate(peers):
            send[p, 0:4] = x[0:4, 256 * j : 256 * j + 256]
            send[p, 4:5] = parts8[j][0:1]

    send_chunks(me, send, got, sems, 4, fill_rows)

    up.wait()
    down.wait()
    table[0:8] = split_table(jnp.where(me == 0, 0.0, halo[0]))
    table[8:136] = own[...]
    table[136:144] = split_table(jnp.where(me == DEVICES - 1, 0.0, halo[1]))
    loads[5].wait()
    loads[6].wait()
    elem_blocks(table, mats, nodes, stiff, *SHARE_ROWS)
    wait_copies(got, DEVICES, sems, 4)

    loads[7].wait()
    loads[8].wait()
    sum_rows(got, left, near, row_acc, near_out, part_ref)
    for k in range(1, fems):
        remote(part_ref, parts.at[f], sems, 6, (lax.rem(f + k, fems), b)).start()
    parts[f] = part_ref[...]
    elem_blocks(table, mats, nodes, stiff, *SHARE_COUPLING)
    wait_copies(parts, fems, sems, 6)

    loads[9].wait()
    far_field(parts, right, shares)
    shares[b] = shares[b] + near_out[...]
    for k in range(1, bems):
        peer = lax.rem(b + k, bems)
        remote(shares.at[peer], sums.at[b], sems, 8, (f, peer)).start()
    sums[b] = shares[b]
    elem_blocks(table, mats, nodes, stiff, *SHARE_FLUX)
    wait_copies(sums, bems, sems, 8)

    loads[10].wait()
    flux = bem_ref[...]
    for k in range(bems):
        flux = flux + sums[k]
    flux_out[...] = flux
    flux_f32[...] = jnp.zeros_like(flux_f32)
    for t in range(9):
        flux_f32[4 * t : 4 * t + 4] = flux[:, 128 * t : 128 * t + 128]
    flux_table[...] = split_table(flux_f32[...])

    def fill_back(peers):
        pos = jnp.concatenate([got[p, 4:5] for p in peers], 1).astype(i32)
        x = pick(flux_table[...], onehot(128, to_bf(pos & 127)), pos >> 7, 5)
        for j, p in enumerate(peers):
            send_back[p] = x[0:4, 256 * j : 256 * j + 256]

    send_chunks(me, send_back, got_back, sems, 10, fill_back)
    elem_blocks(table, mats, nodes, stiff, *SHARE_BACK)
    wait_copies(got_back, DEVICES, sems, 10)

    add_returned(got_back, slots, stiff)
    for q in range(32):
        a = stiff[8 * q : 8 * q + 8]
        fem_out[:, 256 * q : 256 * q + 256] = (a + pltpu.roll(a, 4, axis=0))[0:4]


def whole_call(*args):
    vmem = pl.BlockSpec(memory_space=pltpu.VMEM)
    hbm = pl.BlockSpec(memory_space=pl.ANY)
    rows, elems = args[2].shape[1], args[8].shape[1]
    return pl.pallas_call(
        whole_kernel,
        in_specs=[pl.BlockSpec(memory_space=pltpu.SMEM)] + [hbm] * 11,
        out_specs=[vmem] * 2,
        out_shape=[jax.ShapeDtypeStruct((4, 8192), f32), jax.ShapeDtypeStruct((4, 1152), f32)],
        scratch_shapes=[
            pltpu.VMEM((4, 8192), f32),
            pltpu.VMEM((1, rows), i32),
            pltpu.VMEM((1, rows), i32),
            pltpu.VMEM((1, rows), i32),
            pltpu.VMEM((1, rows), f32),
            pltpu.VMEM((4, 1152), f32),
            pltpu.VMEM((128, 256), f32),
            pltpu.VMEM((4, 4, elems), f32),
            pltpu.VMEM((4, elems), i32),
            pltpu.VMEM((512, 1152), bf16),
            pltpu.VMEM((9, 128, 128), bf16),
            pltpu.VMEM((512, 1152), bf16),
            pltpu.VMEM((1024, 256), f32),
            pltpu.VMEM((DEVICES, 8, 256), f32),
            pltpu.VMEM((144, 512), bf16),
            pltpu.VMEM((128, 512), bf16),
            pltpu.VMEM((2, 8, 256), f32),
            pltpu.VMEM((DEVICES, 5, 256), f32),
            pltpu.VMEM((DEVICES, 5, 256), f32),
            pltpu.VMEM((80, 128), f32),
            pltpu.VMEM((4, 512), f32),
            pltpu.VMEM((4, 1152), f32),
            pltpu.VMEM((8, 4, 512), f32),
            pltpu.VMEM((16, 4, 1152), f32),
            pltpu.VMEM((16, 4, 1152), f32),
            pltpu.VMEM((40, 128), f32),
            pltpu.VMEM((40, 256), bf16),
            pltpu.VMEM((DEVICES, 4, 256), f32),
            pltpu.VMEM((DEVICES, 4, 256), f32),
            pltpu.VMEM((256, 256), f32),
            pltpu.SemaphoreType.DMA((12,)),
            pltpu.SemaphoreType.DMA((11,)),
        ],
        compiler_params=pltpu.CompilerParams(
            collective_id=0, has_side_effects=True, vmem_limit_bytes=VMEM_LIMIT
        ),
        name="whole",
    )(*args)


def per_device(
    fem_field,
    elem_mats,
    elem_nodes,
    trace_count,
    trace_node,
    trace_block,
    trace_pos,
    trace_weight,
    near_tiles,
    left_basis,
    right_basis,
    bem_field,
):
    out, flux = whole_call(
        trace_count,
        fem_field,
        trace_node.reshape(1, -1),
        trace_block.reshape(1, -1),
        trace_pos.reshape(1, -1),
        trace_weight.reshape(1, -1),
        bem_field[0],
        elem_mats,
        elem_nodes,
        left_basis.reshape(512, 1152),
        near_tiles[0],
        right_basis.reshape(512, 1152),
    )
    return out, flux[None]


def solution(mesh):
    placed = (
        P(None, ("fem", "bem")),
        P(None, None, ("fem", "bem")),
        P(None, ("fem", "bem")),
        P(("fem", "bem")),
        P(("fem", "bem")),
        P(("fem", "bem"), None),
        P(("fem", "bem")),
        P(("fem", "bem")),
        P("bem", "fem", None, None),
        P("bem", None, None, "fem"),
        P("bem", None, None, "fem"),
        P("bem", None, "fem"),
    )
    return jax.shard_map(
        per_device,
        mesh=mesh,
        in_specs=placed,
        out_specs=(P(None, ("fem", "bem")), P("bem", None, "fem")),
        check_vma=False,
    )
```

```python
import functools

import jax
import jax.numpy as jnp
from jax import lax
from jax.experimental import pallas as pl
from jax.experimental.pallas import tpu as pltpu
from jax.sharding import PartitionSpec as P

ELEM_BLOCK = 2048
ROW_BLOCK = 4096
SHARE_ROWS = (0, 6)
SHARE_COUPLING = (6, 2)
SHARE_FLUX = (8, 3)
SHARE_BACK = (11, 5)
bf16 = jnp.bfloat16
f32 = jnp.float32
i32 = jnp.int32
MESH = pl.DeviceIdType.MESH
NT = (((1,), (1,)), ((), ()))
VMEM_LIMIT = 63 << 20


def iota(shape, dim):
    return lax.broadcasted_iota(i32, shape, dim)


def to_bf(x):
    return x.astype(f32).astype(bf16)


def onehot(rows, index):
    shape = (rows, index.shape[1])
    return jnp.where(
        to_bf(iota(shape, 0)) == jnp.broadcast_to(index, shape),
        jnp.ones((), bf16),
        jnp.zeros((), bf16),
    )


def split8(x):
    hi = x.astype(bf16).astype(f32)
    return jnp.where(iota(x.shape, 0) < 4, hi, x - hi)


def split_table(t):
    hi = t.astype(bf16)
    return jnp.concatenate([hi, (t - hi.astype(f32)).astype(bf16)], 1)


def pick(table, hot, q, groups):
    r = jnp.dot(table, jnp.concatenate([hot, hot], 0), preferred_element_type=f32)
    shape = (8, hot.shape[1])
    qh = jnp.broadcast_to(q, shape) - jnp.where(iota(shape, 0) >= 4, 1, 0)
    acc = jnp.where(qh == 0, r[0:8], 0.0)
    for j in range(1, groups):
        acc = jnp.where(qh == 2 * j, r[8 * j : 8 * j + 8], acc)
    return acc + pltpu.roll(acc, 4, axis=0)


def spread(part, q, groups):
    part = part.astype(bf16)
    p16 = jnp.concatenate([part, part], 0)
    qv = to_bf(jnp.broadcast_to(q, p16.shape) - jnp.where(iota(p16.shape, 0) >= 8, 1, 0))
    zero = jnp.zeros((), bf16)
    return jnp.concatenate(
        [jnp.where(qv == jnp.asarray(2 * j, bf16), p16, zero) for j in range(groups)], 0
    )


def elem_blocks(table, mats_ref, nodes_ref, out_ref, first, blocks):
    @pl.loop(first, first + blocks)
    def _(i):
        at = pl.ds(pl.multiple_of(i * ELEM_BLOCK, ELEM_BLOCK), ELEM_BLOCK)
        nodes = nodes_ref[:, at]
        hots, xs = [], []
        for a in range(4):
            n = nodes[a : a + 1]
            hot = onehot(256, to_bf(n & 255))
            hots.append(hot)
            xs.append(pick(table[...], hot, n >> 8, 18))
        total = None
        for b in range(4):
            c = mats_ref[0, pl.ds(b, 1), at] * xs[0]
            for a in range(1, 4):
                c = c + mats_ref[a, pl.ds(b, 1), at] * xs[a]
            d = lax.dot_general(
                spread(split8(c), (nodes[b : b + 1] >> 8) - 2, 16),
                hots[b],
                NT,
                preferred_element_type=f32,
            )
            total = d if total is None else total + d
        out_ref[...] += total


def coded(exponent, mantissa, negative):
    size = ((mantissa + 128) << exponent).astype(f32)
    return jnp.where(negative, -size, size)


def bucket_rows(count_ref, node_ref, block_ref, pos_ref, weight_ref, out_ref, acc, meanwhile):
    rb = ROW_BLOCK
    acc[...] = jnp.zeros_like(acc)

    def step(i, before):
        meanwhile(i)
        at = pl.ds(pl.multiple_of(i * rb, rb), rb)
        node, pos, block = node_ref[:, at], pos_ref[:, at], block_ref[:, at]
        row = i * rb + iota((1, rb), 1)
        coef = jnp.where(row < count_ref[0], weight_ref[:, at], 0.0)
        bucket = (block & 7) * 16 + (block >> 3)

        owner = onehot(128, to_bf(bucket))
        upper = jnp.where(iota((256, 256), 0) <= iota((256, 256), 1), 1.0, 0.0).astype(bf16)
        ranks = []
        for k in range(0, rb, 256):
            hot = owner[:, k : k + 256]
            counts = jnp.dot(hot, upper, preferred_element_type=f32) + before
            ranks.append(jnp.sum(hot.astype(f32) * counts, axis=0, keepdims=True) - 1.0)
            before = counts[:, 255:256]
        slot = onehot(256, jnp.concatenate(ranks, 1).astype(bf16))

        hi = coef.astype(bf16).astype(f32)
        first = coded(pos >> 7, pos & 127, (node & 4096) > 0)
        second = coded((node >> 7) & 15, node & 127, (node & 2048) > 0)
        sub = iota((16, rb), 0) & 3
        part = jnp.broadcast_to(coef - hi, (16, rb))
        for k, item in enumerate((first, second, hi)):
            part = jnp.where(sub == k, jnp.broadcast_to(item, (16, rb)), part)
        part = part.astype(bf16)
        at16 = to_bf(jnp.broadcast_to(bucket, (16, rb)) - (iota((16, rb), 0) >> 2))
        zero = jnp.zeros((), bf16)
        spread4 = jnp.concatenate(
            [jnp.where(at16 == jnp.asarray(4 * j, bf16), part, zero) for j in range(32)], 0
        )
        acc[...] += lax.dot_general(spread4, slot, NT, preferred_element_type=f32)
        return before

    lax.fori_loop(0, node_ref.shape[1] // rb, step, jnp.zeros((128, 1), f32))

    rows = 64

    @pl.loop(0, 512 // rows)
    def _(i):
        v = acc[pl.ds(pl.multiple_of(i * rows, rows), rows), :]
        size = jnp.abs(v)
        sign = jnp.where(v < 0, 1.0, 0.0)
        e = jnp.zeros(v.shape, i32)
        for k in range(1, 16):
            e = e + jnp.where(size >= 128.0 * 2**k, 1, 0)
        code = ((e << 7) + (size.astype(i32) >> e) - 128).astype(f32)
        kind = iota(v.shape, 0) & 3
        node = code + 2048.0 * sign + 4096.0 * pltpu.roll(sign, 1, axis=0)
        coef = v + pltpu.roll(v, rows - 1, axis=0)
        out = jnp.where(kind == 0, code, jnp.where(kind == 1, node, coef))
        for j in range(rows // 8):
            tile = out[8 * j : 8 * j + 8]
            out_ref[i * (rows // 4) + 2 * j] = tile
            out_ref[i * (rows // 4) + 2 * j + 1] = pltpu.roll(tile, 4, axis=0)


DEVICES = 128


def place(index):
    wide = lax.axis_size("bem")
    return (index // wide, lax.rem(index, wide))


def greet(me, first, count):
    barrier = pltpu.get_barrier_semaphore()
    for k in range(count):
        peer = lax.rem(me + first + k, DEVICES)
        pl.semaphore_signal(barrier, inc=1, device_id=place(peer), device_id_type=MESH)


def await_all():
    pl.semaphore_wait(pltpu.get_barrier_semaphore(), DEVICES - 1)


def remote(src, dst, sems, at, device):
    return pltpu.make_async_remote_copy(
        src_ref=src,
        dst_ref=dst,
        send_sem=sems.at[at],
        recv_sem=sems.at[at + 1],
        device_id=device,
        device_id_type=MESH,
    )


def wait_bytes(ref, sem):
    pltpu.make_async_copy(ref, ref, sem).wait()


def send_chunks(me, send, got, sems, at, fill):
    group = 16

    def chunk(i, last):
        peers = [lax.rem(me + i * group + j + 1, DEVICES) for j in range(group)]
        fill(peers)
        for peer in peers[: group - 1] if last else peers:
            remote(send.at[peer], got.at[me], sems, at, place(peer)).start()

    @pl.loop(0, DEVICES // group - 1)
    def _(i):
        chunk(i, False)

    chunk(DEVICES // group - 1, True)
    got[me] = send[me]


def wait_copies(ref, count, sems, at):
    most = ref.at[pl.ds(0, count - 1)]
    wait_bytes(most, sems.at[at])
    wait_bytes(most, sems.at[at + 1])


def sum_rows(got, left, near, acc, near_out, part_ref):
    acc[...] = jnp.zeros_like(acc)
    group = 16

    @pl.loop(0, DEVICES // group)
    def _(i):
        tiles = [got[i * group + j] for j in range(group)]
        vals = jnp.concatenate([t[0:4] for t in tiles], 1)
        pos = jnp.concatenate([t[4:5] for t in tiles], 1).astype(i32)
        acc[...] += lax.dot_general(
            spread(split8(jnp.concatenate([vals, vals], 0)), pos >> 7, 5),
            onehot(128, to_bf(pos & 127)),
            NT,
            preferred_element_type=f32,
        )

    pieces = []
    for t in range(9):
        a = acc[8 * t : 8 * t + 8]
        piece = split8(a + pltpu.roll(a, 4, axis=0)).astype(bf16)
        pieces.append(piece)
        n = jnp.dot(piece, near[t], preferred_element_type=f32)
        near_out[:, 128 * t : 128 * t + 128] = (n + pltpu.roll(n, 4, axis=0))[0:4]
    c = lax.dot_general(jnp.concatenate(pieces, 1), left[...], NT, preferred_element_type=f32)
    part_ref[...] = (c + pltpu.roll(c, 4, axis=0))[0:4]


def far_field(parts, right, shares):
    total = parts[0]
    for k in range(1, parts.shape[0]):
        total = total + parts[k]
    for half in range(2):
        c = total[:, 256 * half : 256 * half + 256]
        c = split8(jnp.concatenate([c, c], 0))
        stacked = jnp.concatenate([c] * 8, 0)
        shape = stacked.shape
        diag = jnp.where((iota(shape, 0) >> 3) == (iota(shape, 1) >> 5), stacked, 0.0).astype(bf16)
        far = jnp.dot(diag, right[256 * half : 256 * half + 256], preferred_element_type=f32)
        for s in range(8):
            a = far[8 * s : 8 * s + 8]
            shares[8 * half + s] = (a + pltpu.roll(a, 4, axis=0))[0:4]


def add_returned(got, slots, acc):
    group = 16

    @pl.loop(0, DEVICES // group)
    def _(i):
        at = [i * group + j for j in range(group)]
        node = jnp.concatenate([slots[s, 1:2] for s in at], 1).astype(i32)
        coef = jnp.concatenate([slots[s, 2:3] for s in at], 1)
        x = jnp.concatenate([got[s] for s in at], 1)
        x = jnp.concatenate([x, x], 0) * coef
        acc[...] += lax.dot_general(
            spread(split8(x), node >> 8, 16),
            onehot(256, to_bf(node & 255)),
            NT,
            preferred_element_type=f32,
        )


def whole_kernel(
    count_ref,
    field_hbm,
    node_hbm,
    block_hbm,
    pos_hbm,
    weight_hbm,
    bem_hbm,
    mats_hbm,
    nodes_hbm,
    left_hbm,
    near_hbm,
    right_hbm,
    stiff,
    flux_out,
    field,
    node_ref,
    block_ref,
    pos_ref,
    weight_ref,
    bem_ref,
    field_ref,
    mats,
    nodes,
    left,
    near,
    right,
    bucket_acc,
    slots,
    table,
    own,
    halo,
    send,
    got,
    row_acc,
    part_ref,
    near_out,
    parts,
    shares,
    sums,
    flux_f32,
    flux_table,
    send_back,
    got_back,
    sems,
    local_sems,
):
    fems, bems = lax.axis_size("fem"), lax.axis_size("bem")
    f, b = lax.axis_index("fem"), lax.axis_index("bem")
    me = f * bems + b
    pairs = [
        (block_hbm, block_ref),
        (node_hbm, node_ref),
        (pos_hbm, pos_ref),
        (weight_hbm, weight_ref),
        (field_hbm, field),
        (nodes_hbm, nodes),
        (mats_hbm, mats),
        (left_hbm, left),
        (near_hbm, near),
        (right_hbm, right),
        (bem_hbm, bem_ref),
    ]
    loads = [
        pltpu.make_async_copy(src, dst, local_sems.at[k]) for k, (src, dst) in enumerate(pairs)
    ]
    for load in loads:
        load.start()
    greet(me, 1, 7)
    stiff[...] = jnp.zeros_like(stiff)
    for load in loads[:4]:
        load.wait()
    steps = node_ref.shape[1] // ROW_BLOCK
    share = (DEVICES - 8) // steps
    bucket_rows(
        count_ref,
        node_ref,
        block_ref,
        pos_ref,
        weight_ref,
        slots,
        bucket_acc,
        lambda i: greet(me, 8 + i * share, share),
    )
    loads[4].wait()
    for q in range(32):
        field_ref[4 * q : 4 * q + 4] = field[:, 256 * q : 256 * q + 256]
    own[...] = split_table(field_ref[...])

    await_all()
    up = remote(
        field_ref.at[pl.ds(120, 8)], halo.at[0], sems, 0, place(lax.rem(me + 1, DEVICES))
    )
    down = remote(
        field_ref.at[pl.ds(0, 8)], halo.at[1], sems, 2, place(lax.rem(me + DEVICES - 1, DEVICES))
    )
    up.start()
    down.start()

    def fill_rows(peers):
        parts8 = [slots[p] for p in peers]
        node = jnp.concatenate([t[1:2] for t in parts8], 1).astype(i32)
        coef = jnp.concatenate([t[2:3] for t in parts8], 1)
        x = pick(own[...], onehot(256, to_bf(node & 255)), node >> 8, 16) * coef
        for j, p in enumerate(peers):
            send[p, 0:4] = x[0:4, 256 * j : 256 * j + 256]
            send[p, 4:5] = parts8[j][0:1]

    send_chunks(me, send, got, sems, 4, fill_rows)

    up.wait()
    down.wait()
    table[0:8] = split_table(jnp.where(me == 0, 0.0, halo[0]))
    table[8:136] = own[...]
    table[136:144] = split_table(jnp.where(me == DEVICES - 1, 0.0, halo[1]))
    loads[5].wait()
    loads[6].wait()
    elem_blocks(table, mats, nodes, stiff, *SHARE_ROWS)
    wait_copies(got, DEVICES, sems, 4)

    loads[7].wait()
    loads[8].wait()
    sum_rows(got, left, near, row_acc, near_out, part_ref)
    for k in range(1, fems):
        remote(part_ref, parts.at[f], sems, 6, (lax.rem(f + k, fems), b)).start()
    parts[f] = part_ref[...]
    elem_blocks(table, mats, nodes, stiff, *SHARE_COUPLING)
    wait_copies(parts, fems, sems, 6)

    loads[9].wait()
    far_field(parts, right, shares)
    shares[b] = shares[b] + near_out[...]
    for k in range(1, bems):
        peer = lax.rem(b + k, bems)
        remote(shares.at[peer], sums.at[b], sems, 8, (f, peer)).start()
    sums[b] = shares[b]
    elem_blocks(table, mats, nodes, stiff, *SHARE_FLUX)
    wait_copies(sums, bems, sems, 8)

    loads[10].wait()
    flux = bem_ref[...]
    for k in range(bems):
        flux = flux + sums[k]
    flux_out[...] = flux
    flux_f32[...] = jnp.zeros_like(flux_f32)
    for t in range(9):
        flux_f32[4 * t : 4 * t + 4] = flux[:, 128 * t : 128 * t + 128]
    flux_table[...] = split_table(flux_f32[...])

    def fill_back(peers):
        pos = jnp.concatenate([got[p, 4:5] for p in peers], 1).astype(i32)
        x = pick(flux_table[...], onehot(128, to_bf(pos & 127)), pos >> 7, 5)
        for j, p in enumerate(peers):
            send_back[p] = x[0:4, 256 * j : 256 * j + 256]

    send_chunks(me, send_back, got_back, sems, 10, fill_back)
    elem_blocks(table, mats, nodes, stiff, *SHARE_BACK)
    wait_copies(got_back, DEVICES, sems, 10)

    add_returned(got_back, slots, stiff)


def whole_call(*args):
    vmem = pl.BlockSpec(memory_space=pltpu.VMEM)
    hbm = pl.BlockSpec(memory_space=pl.ANY)
    rows, elems = args[2].shape[1], args[8].shape[1]
    return pl.pallas_call(
        whole_kernel,
        in_specs=[pl.BlockSpec(memory_space=pltpu.SMEM)] + [hbm] * 11,
        out_specs=[vmem] * 2,
        out_shape=[jax.ShapeDtypeStruct((256, 256), f32), jax.ShapeDtypeStruct((4, 1152), f32)],
        scratch_shapes=[
            pltpu.VMEM((4, 8192), f32),
            pltpu.VMEM((1, rows), i32),
            pltpu.VMEM((1, rows), i32),
            pltpu.VMEM((1, rows), i32),
            pltpu.VMEM((1, rows), f32),
            pltpu.VMEM((4, 1152), f32),
            pltpu.VMEM((128, 256), f32),
            pltpu.VMEM((4, 4, elems), f32),
            pltpu.VMEM((4, elems), i32),
            pltpu.VMEM((512, 1152), bf16),
            pltpu.VMEM((9, 128, 128), bf16),
            pltpu.VMEM((512, 1152), bf16),
            pltpu.VMEM((512, 256), f32),
            pltpu.VMEM((DEVICES, 8, 256), f32),
            pltpu.VMEM((144, 512), bf16),
            pltpu.VMEM((128, 512), bf16),
            pltpu.VMEM((2, 8, 256), f32),
            pltpu.VMEM((DEVICES, 5, 256), f32),
            pltpu.VMEM((DEVICES, 5, 256), f32),
            pltpu.VMEM((80, 128), f32),
            pltpu.VMEM((4, 512), f32),
            pltpu.VMEM((4, 1152), f32),
            pltpu.VMEM((8, 4, 512), f32),
            pltpu.VMEM((16, 4, 1152), f32),
            pltpu.VMEM((16, 4, 1152), f32),
            pltpu.VMEM((40, 128), f32),
            pltpu.VMEM((40, 256), bf16),
            pltpu.VMEM((DEVICES, 4, 256), f32),
            pltpu.VMEM((DEVICES, 4, 256), f32),
            pltpu.SemaphoreType.DMA((12,)),
            pltpu.SemaphoreType.DMA((11,)),
        ],
        compiler_params=pltpu.CompilerParams(
            collective_id=0, has_side_effects=True, vmem_limit_bytes=VMEM_LIMIT
        ),
        name="whole",
    )(*args)


def finish_kernel(parts_ref, flux_ref, fem_out, flux_out):
    flux_out[0] = flux_ref[...]
    for q in range(32):
        a = parts_ref[8 * q : 8 * q + 8]
        fem_out[:, 256 * q : 256 * q + 256] = (a + pltpu.roll(a, 4, axis=0))[0:4]


def finish_call(parts, flux):
    vmem = pl.BlockSpec(memory_space=pltpu.VMEM)
    return pl.pallas_call(
        finish_kernel,
        in_specs=[vmem] * 2,
        out_specs=[vmem] * 2,
        out_shape=[jax.ShapeDtypeStruct((4, 8192), f32), jax.ShapeDtypeStruct((1, 4, 1152), f32)],
        compiler_params=pltpu.CompilerParams(vmem_limit_bytes=VMEM_LIMIT),
        name="finish",
    )(parts, flux)


def per_device(
    fem_field,
    elem_mats,
    elem_nodes,
    trace_count,
    trace_node,
    trace_block,
    trace_pos,
    trace_weight,
    near_tiles,
    left_basis,
    right_basis,
    bem_field,
):
    parts, flux = whole_call(
        trace_count,
        fem_field,
        trace_node.reshape(1, -1),
        trace_block.reshape(1, -1),
        trace_pos.reshape(1, -1),
        trace_weight.reshape(1, -1),
        bem_field[0],
        elem_mats,
        elem_nodes,
        left_basis.reshape(512, 1152),
        near_tiles[0],
        right_basis.reshape(512, 1152),
    )
    return finish_call(parts, flux)


def solution(mesh):
    placed = (
        P(None, ("fem", "bem")),
        P(None, None, ("fem", "bem")),
        P(None, ("fem", "bem")),
        P(("fem", "bem")),
        P(("fem", "bem")),
        P(("fem", "bem"), None),
        P(("fem", "bem")),
        P(("fem", "bem")),
        P("bem", "fem", None, None),
        P("bem", None, None, "fem"),
        P("bem", None, None, "fem"),
        P("bem", None, "fem"),
    )
    return jax.shard_map(
        per_device,
        mesh=mesh,
        in_specs=placed,
        out_specs=(P(None, ("fem", "bem")), P("bem", None, "fem")),
        check_vma=False,
    )
```

```python
import functools

import jax
import jax.numpy as jnp
from jax import lax
from jax.experimental import pallas as pl
from jax.experimental.pallas import tpu as pltpu
from jax.sharding import PartitionSpec as P

ELEM_BLOCK = 4096
ROW_BLOCK = 8192
SHARE_ROWS = (0, 3)
SHARE_COUPLING = (3, 1)
SHARE_FLUX = (4, 2)
SHARE_BACK = (6, 2)
bf16 = jnp.bfloat16
f32 = jnp.float32
i32 = jnp.int32
MESH = pl.DeviceIdType.MESH
NT = (((1,), (1,)), ((), ()))
VMEM_LIMIT = 63 << 20


def iota(shape, dim):
    return lax.broadcasted_iota(i32, shape, dim)


def to_bf(x):
    return x.astype(f32).astype(bf16)


def onehot(rows, index):
    shape = (rows, index.shape[1])
    return jnp.where(
        to_bf(iota(shape, 0)) == jnp.broadcast_to(index, shape),
        jnp.ones((), bf16),
        jnp.zeros((), bf16),
    )


def split8(x):
    hi = x.astype(bf16).astype(f32)
    return jnp.where(iota(x.shape, 0) < 4, hi, x - hi)


def split_table(t):
    hi = t.astype(bf16)
    return jnp.concatenate([hi, (t - hi.astype(f32)).astype(bf16)], 1)


def pick(table, hot, q, groups):
    r = jnp.dot(table, jnp.concatenate([hot, hot], 0), preferred_element_type=f32)
    shape = (8, hot.shape[1])
    qh = jnp.broadcast_to(q, shape) - jnp.where(iota(shape, 0) >= 4, 1, 0)
    acc = jnp.where(qh == 0, r[0:8], 0.0)
    for j in range(1, groups):
        acc = jnp.where(qh == 2 * j, r[8 * j : 8 * j + 8], acc)
    return acc + pltpu.roll(acc, 4, axis=0)


def spread(part, q, groups):
    part = part.astype(bf16)
    p16 = jnp.concatenate([part, part], 0)
    qv = to_bf(jnp.broadcast_to(q, p16.shape) - jnp.where(iota(p16.shape, 0) >= 8, 1, 0))
    zero = jnp.zeros((), bf16)
    return jnp.concatenate(
        [jnp.where(qv == jnp.asarray(2 * j, bf16), p16, zero) for j in range(groups)], 0
    )


def elem_blocks(table, mats_ref, nodes_ref, out_ref, first, blocks):
    @pl.loop(first, first + blocks)
    def _(i):
        at = pl.ds(pl.multiple_of(i * ELEM_BLOCK, ELEM_BLOCK), ELEM_BLOCK)
        nodes = nodes_ref[:, at]
        hots, xs = [], []
        for a in range(4):
            n = nodes[a : a + 1]
            hot = onehot(256, to_bf(n & 255))
            hots.append(hot)
            xs.append(pick(table[...], hot, n >> 8, 18))
        total = None
        for b in range(4):
            c = mats_ref[0, pl.ds(b, 1), at] * xs[0]
            for a in range(1, 4):
                c = c + mats_ref[a, pl.ds(b, 1), at] * xs[a]
            d = lax.dot_general(
                spread(split8(c), (nodes[b : b + 1] >> 8) - 2, 16),
                hots[b],
                NT,
                preferred_element_type=f32,
            )
            total = d if total is None else total + d
        out_ref[...] += total


def coded(exponent, mantissa, negative):
    size = ((mantissa + 128) << exponent).astype(f32)
    return jnp.where(negative, -size, size)


def bucket_rows(count_ref, node_ref, block_ref, pos_ref, weight_ref, out_ref, acc, meanwhile):
    rb = ROW_BLOCK
    acc[...] = jnp.zeros_like(acc)

    def step(i, before):
        meanwhile(i)
        at = pl.ds(pl.multiple_of(i * rb, rb), rb)
        node, pos, block = node_ref[:, at], pos_ref[:, at], block_ref[:, at]
        row = i * rb + iota((1, rb), 1)
        coef = jnp.where(row < count_ref[0], weight_ref[:, at], 0.0)
        bucket = (block & 7) * 16 + (block >> 3)

        owner = onehot(128, to_bf(bucket))
        upper = jnp.where(iota((256, 256), 0) <= iota((256, 256), 1), 1.0, 0.0).astype(bf16)
        ranks = []
        for k in range(0, rb, 256):
            hot = owner[:, k : k + 256]
            counts = jnp.dot(hot, upper, preferred_element_type=f32) + before
            ranks.append(jnp.sum(hot.astype(f32) * counts, axis=0, keepdims=True) - 1.0)
            before = counts[:, 255:256]
        slot = onehot(256, jnp.concatenate(ranks, 1).astype(bf16))

        hi = coef.astype(bf16).astype(f32)
        first = coded(pos >> 7, pos & 127, (node & 4096) > 0)
        second = coded((node >> 7) & 15, node & 127, (node & 2048) > 0)
        sub = iota((16, rb), 0) & 3
        part = jnp.broadcast_to(coef - hi, (16, rb))
        for k, item in enumerate((first, second, hi)):
            part = jnp.where(sub == k, jnp.broadcast_to(item, (16, rb)), part)
        part = part.astype(bf16)
        at16 = to_bf(jnp.broadcast_to(bucket, (16, rb)) - (iota((16, rb), 0) >> 2))
        zero = jnp.zeros((), bf16)
        spread4 = jnp.concatenate(
            [jnp.where(at16 == jnp.asarray(4 * j, bf16), part, zero) for j in range(32)], 0
        )
        acc[...] += lax.dot_general(spread4, slot, NT, preferred_element_type=f32)
        return before

    lax.fori_loop(0, node_ref.shape[1] // rb, step, jnp.zeros((128, 1), f32))

    rows = 64

    @pl.loop(0, 512 // rows)
    def _(i):
        v = acc[pl.ds(pl.multiple_of(i * rows, rows), rows), :]
        size = jnp.abs(v)
        sign = jnp.where(v < 0, 1.0, 0.0)
        e = jnp.zeros(v.shape, i32)
        for k in range(1, 16):
            e = e + jnp.where(size >= 128.0 * 2**k, 1, 0)
        code = ((e << 7) + (size.astype(i32) >> e) - 128).astype(f32)
        kind = iota(v.shape, 0) & 3
        node = code + 2048.0 * sign + 4096.0 * pltpu.roll(sign, 1, axis=0)
        coef = v + pltpu.roll(v, rows - 1, axis=0)
        out = jnp.where(kind == 0, code, jnp.where(kind == 1, node, coef))
        for j in range(rows // 8):
            tile = out[8 * j : 8 * j + 8]
            out_ref[i * (rows // 4) + 2 * j] = tile
            out_ref[i * (rows // 4) + 2 * j + 1] = pltpu.roll(tile, 4, axis=0)


DEVICES = 128


def place(index):
    wide = lax.axis_size("bem")
    return (index // wide, lax.rem(index, wide))


def greet(me, first, count):
    barrier = pltpu.get_barrier_semaphore()
    for k in range(count):
        peer = lax.rem(me + first + k, DEVICES)
        pl.semaphore_signal(barrier, inc=1, device_id=place(peer), device_id_type=MESH)


def await_all():
    pl.semaphore_wait(pltpu.get_barrier_semaphore(), DEVICES - 1)


def remote(src, dst, sems, at, device):
    return pltpu.make_async_remote_copy(
        src_ref=src,
        dst_ref=dst,
        send_sem=sems.at[at],
        recv_sem=sems.at[at + 1],
        device_id=device,
        device_id_type=MESH,
    )


def wait_bytes(ref, sem):
    pltpu.make_async_copy(ref, ref, sem).wait()


def send_chunks(me, send, got, sems, at, fill):
    group = 16

    def chunk(i, last):
        peers = [lax.rem(me + i * group + j + 1, DEVICES) for j in range(group)]
        fill(peers)
        for peer in peers[: group - 1] if last else peers:
            remote(send.at[peer], got.at[me], sems, at, place(peer)).start()

    @pl.loop(0, DEVICES // group - 1)
    def _(i):
        chunk(i, False)

    chunk(DEVICES // group - 1, True)
    got[me] = send[me]


def wait_copies(ref, count, sems, at):
    most = ref.at[pl.ds(0, count - 1)]
    wait_bytes(most, sems.at[at])
    wait_bytes(most, sems.at[at + 1])


def sum_rows(got, left, near, acc, near_out, part_ref):
    acc[...] = jnp.zeros_like(acc)
    group = 32

    @pl.loop(0, DEVICES // group)
    def _(i):
        tiles = [got[i * group + j] for j in range(group)]
        vals = jnp.concatenate([t[0:4] for t in tiles], 1)
        pos = jnp.concatenate([t[4:5] for t in tiles], 1).astype(i32)
        acc[...] += lax.dot_general(
            spread(split8(jnp.concatenate([vals, vals], 0)), pos >> 7, 5),
            onehot(128, to_bf(pos & 127)),
            NT,
            preferred_element_type=f32,
        )

    pieces = []
    for t in range(9):
        a = acc[8 * t : 8 * t + 8]
        piece = split8(a + pltpu.roll(a, 4, axis=0)).astype(bf16)
        pieces.append(piece)
        n = jnp.dot(piece, near[t], preferred_element_type=f32)
        near_out[:, 128 * t : 128 * t + 128] = (n + pltpu.roll(n, 4, axis=0))[0:4]
    c = lax.dot_general(jnp.concatenate(pieces, 1), left[...], NT, preferred_element_type=f32)
    part_ref[...] = (c + pltpu.roll(c, 4, axis=0))[0:4]


def far_field(parts, right, shares):
    total = parts[0]
    for k in range(1, parts.shape[0]):
        total = total + parts[k]
    for half in range(2):
        c = total[:, 256 * half : 256 * half + 256]
        c = split8(jnp.concatenate([c, c], 0))
        stacked = jnp.concatenate([c] * 8, 0)
        shape = stacked.shape
        diag = jnp.where((iota(shape, 0) >> 3) == (iota(shape, 1) >> 5), stacked, 0.0).astype(bf16)
        far = jnp.dot(diag, right[256 * half : 256 * half + 256], preferred_element_type=f32)
        for s in range(8):
            a = far[8 * s : 8 * s + 8]
            shares[8 * half + s] = (a + pltpu.roll(a, 4, axis=0))[0:4]


def add_returned(got, slots, acc):
    group = 32

    @pl.loop(0, DEVICES // group)
    def _(i):
        at = [i * group + j for j in range(group)]
        node = jnp.concatenate([slots[s, 1:2] for s in at], 1).astype(i32)
        coef = jnp.concatenate([slots[s, 2:3] for s in at], 1)
        x = jnp.concatenate([got[s] for s in at], 1)
        x = jnp.concatenate([x, x], 0) * coef
        acc[...] += lax.dot_general(
            spread(split8(x), node >> 8, 16),
            onehot(256, to_bf(node & 255)),
            NT,
            preferred_element_type=f32,
        )


def whole_kernel(
    count_ref,
    field_hbm,
    node_hbm,
    block_hbm,
    pos_hbm,
    weight_hbm,
    bem_hbm,
    mats_hbm,
    nodes_hbm,
    left_hbm,
    near_hbm,
    right_hbm,
    stiff,
    flux_out,
    field,
    node_ref,
    block_ref,
    pos_ref,
    weight_ref,
    bem_ref,
    field_ref,
    mats,
    nodes,
    left,
    near,
    right,
    bucket_acc,
    slots,
    table,
    own,
    halo,
    send,
    got,
    row_acc,
    part_ref,
    near_out,
    parts,
    shares,
    sums,
    flux_f32,
    flux_table,
    send_back,
    got_back,
    sems,
    local_sems,
):
    fems, bems = lax.axis_size("fem"), lax.axis_size("bem")
    f, b = lax.axis_index("fem"), lax.axis_index("bem")
    me = f * bems + b
    pairs = [
        (block_hbm, block_ref),
        (node_hbm, node_ref),
        (pos_hbm, pos_ref),
        (weight_hbm, weight_ref),
        (field_hbm, field),
        (nodes_hbm, nodes),
        (mats_hbm, mats),
        (left_hbm, left),
        (near_hbm, near),
        (right_hbm, right),
        (bem_hbm, bem_ref),
    ]
    loads = [
        pltpu.make_async_copy(src, dst, local_sems.at[k]) for k, (src, dst) in enumerate(pairs)
    ]
    for load in loads:
        load.start()
    greet(me, 1, 7)
    stiff[...] = jnp.zeros_like(stiff)
    for load in loads[:4]:
        load.wait()
    steps = node_ref.shape[1] // ROW_BLOCK
    share = (DEVICES - 8) // steps
    bucket_rows(
        count_ref,
        node_ref,
        block_ref,
        pos_ref,
        weight_ref,
        slots,
        bucket_acc,
        lambda i: greet(me, 8 + i * share, share),
    )
    loads[4].wait()
    for q in range(32):
        field_ref[4 * q : 4 * q + 4] = field[:, 256 * q : 256 * q + 256]
    own[...] = split_table(field_ref[...])

    await_all()
    up = remote(
        field_ref.at[pl.ds(120, 8)], halo.at[0], sems, 0, place(lax.rem(me + 1, DEVICES))
    )
    down = remote(
        field_ref.at[pl.ds(0, 8)], halo.at[1], sems, 2, place(lax.rem(me + DEVICES - 1, DEVICES))
    )
    up.start()
    down.start()

    def fill_rows(peers):
        parts8 = [slots[p] for p in peers]
        node = jnp.concatenate([t[1:2] for t in parts8], 1).astype(i32)
        coef = jnp.concatenate([t[2:3] for t in parts8], 1)
        x = pick(own[...], onehot(256, to_bf(node & 255)), node >> 8, 16) * coef
        for j, p in enumerate(peers):
            send[p, 0:4] = x[0:4, 256 * j : 256 * j + 256]
            send[p, 4:5] = parts8[j][0:1]

    send_chunks(me, send, got, sems, 4, fill_rows)

    up.wait()
    down.wait()
    table[0:8] = split_table(jnp.where(me == 0, 0.0, halo[0]))
    table[8:136] = own[...]
    table[136:144] = split_table(jnp.where(me == DEVICES - 1, 0.0, halo[1]))
    loads[5].wait()
    loads[6].wait()
    elem_blocks(table, mats, nodes, stiff, *SHARE_ROWS)
    wait_copies(got, DEVICES, sems, 4)

    loads[7].wait()
    loads[8].wait()
    sum_rows(got, left, near, row_acc, near_out, part_ref)
    for k in range(1, fems):
        remote(part_ref, parts.at[f], sems, 6, (lax.rem(f + k, fems), b)).start()
    parts[f] = part_ref[...]
    elem_blocks(table, mats, nodes, stiff, *SHARE_COUPLING)
    wait_copies(parts, fems, sems, 6)

    loads[9].wait()
    far_field(parts, right, shares)
    shares[b] = shares[b] + near_out[...]
    for k in range(1, bems):
        peer = lax.rem(b + k, bems)
        remote(shares.at[peer], sums.at[b], sems, 8, (f, peer)).start()
    sums[b] = shares[b]
    elem_blocks(table, mats, nodes, stiff, *SHARE_FLUX)
    wait_copies(sums, bems, sems, 8)

    loads[10].wait()
    flux = bem_ref[...]
    for k in range(bems):
        flux = flux + sums[k]
    flux_out[...] = flux
    flux_f32[...] = jnp.zeros_like(flux_f32)
    for t in range(9):
        flux_f32[4 * t : 4 * t + 4] = flux[:, 128 * t : 128 * t + 128]
    flux_table[...] = split_table(flux_f32[...])

    def fill_back(peers):
        pos = jnp.concatenate([got[p, 4:5] for p in peers], 1).astype(i32)
        x = pick(flux_table[...], onehot(128, to_bf(pos & 127)), pos >> 7, 5)
        for j, p in enumerate(peers):
            send_back[p] = x[0:4, 256 * j : 256 * j + 256]

    send_chunks(me, send_back, got_back, sems, 10, fill_back)
    elem_blocks(table, mats, nodes, stiff, *SHARE_BACK)
    wait_copies(got_back, DEVICES, sems, 10)

    add_returned(got_back, slots, stiff)


def whole_call(*args):
    vmem = pl.BlockSpec(memory_space=pltpu.VMEM)
    hbm = pl.BlockSpec(memory_space=pl.ANY)
    rows, elems = args[2].shape[1], args[8].shape[1]
    return pl.pallas_call(
        whole_kernel,
        in_specs=[pl.BlockSpec(memory_space=pltpu.SMEM)] + [hbm] * 11,
        out_specs=[vmem] * 2,
        out_shape=[jax.ShapeDtypeStruct((256, 256), f32), jax.ShapeDtypeStruct((4, 1152), f32)],
        scratch_shapes=[
            pltpu.VMEM((4, 8192), f32),
            pltpu.VMEM((1, rows), i32),
            pltpu.VMEM((1, rows), i32),
            pltpu.VMEM((1, rows), i32),
            pltpu.VMEM((1, rows), f32),
            pltpu.VMEM((4, 1152), f32),
            pltpu.VMEM((128, 256), f32),
            pltpu.VMEM((4, 4, elems), f32),
            pltpu.VMEM((4, elems), i32),
            pltpu.VMEM((512, 1152), bf16),
            pltpu.VMEM((9, 128, 128), bf16),
            pltpu.VMEM((512, 1152), bf16),
            pltpu.VMEM((512, 256), f32),
            pltpu.VMEM((DEVICES, 8, 256), f32),
            pltpu.VMEM((144, 512), bf16),
            pltpu.VMEM((128, 512), bf16),
            pltpu.VMEM((2, 8, 256), f32),
            pltpu.VMEM((DEVICES, 5, 256), f32),
            pltpu.VMEM((DEVICES, 5, 256), f32),
            pltpu.VMEM((80, 128), f32),
            pltpu.VMEM((4, 512), f32),
            pltpu.VMEM((4, 1152), f32),
            pltpu.VMEM((8, 4, 512), f32),
            pltpu.VMEM((16, 4, 1152), f32),
            pltpu.VMEM((16, 4, 1152), f32),
            pltpu.VMEM((40, 128), f32),
            pltpu.VMEM((40, 256), bf16),
            pltpu.VMEM((DEVICES, 4, 256), f32),
            pltpu.VMEM((DEVICES, 4, 256), f32),
            pltpu.SemaphoreType.DMA((12,)),
            pltpu.SemaphoreType.DMA((11,)),
        ],
        compiler_params=pltpu.CompilerParams(
            collective_id=0, has_side_effects=True, vmem_limit_bytes=VMEM_LIMIT
        ),
        name="whole",
    )(*args)


def finish_kernel(parts_ref, flux_ref, fem_out, flux_out):
    flux_out[0] = flux_ref[...]
    for q in range(32):
        a = parts_ref[8 * q : 8 * q + 8]
        fem_out[:, 256 * q : 256 * q + 256] = (a + pltpu.roll(a, 4, axis=0))[0:4]


def finish_call(parts, flux):
    vmem = pl.BlockSpec(memory_space=pltpu.VMEM)
    return pl.pallas_call(
        finish_kernel,
        in_specs=[vmem] * 2,
        out_specs=[vmem] * 2,
        out_shape=[jax.ShapeDtypeStruct((4, 8192), f32), jax.ShapeDtypeStruct((1, 4, 1152), f32)],
        compiler_params=pltpu.CompilerParams(vmem_limit_bytes=VMEM_LIMIT),
        name="finish",
    )(parts, flux)


def per_device(
    fem_field,
    elem_mats,
    elem_nodes,
    trace_count,
    trace_node,
    trace_block,
    trace_pos,
    trace_weight,
    near_tiles,
    left_basis,
    right_basis,
    bem_field,
):
    parts, flux = whole_call(
        trace_count,
        fem_field,
        trace_node.reshape(1, -1),
        trace_block.reshape(1, -1),
        trace_pos.reshape(1, -1),
        trace_weight.reshape(1, -1),
        bem_field[0],
        elem_mats,
        elem_nodes,
        left_basis.reshape(512, 1152),
        near_tiles[0],
        right_basis.reshape(512, 1152),
    )
    return finish_call(parts, flux)


def solution(mesh):
    placed = (
        P(None, ("fem", "bem")),
        P(None, None, ("fem", "bem")),
        P(None, ("fem", "bem")),
        P(("fem", "bem")),
        P(("fem", "bem")),
        P(("fem", "bem"), None),
        P(("fem", "bem")),
        P(("fem", "bem")),
        P("bem", "fem", None, None),
        P("bem", None, None, "fem"),
        P("bem", None, None, "fem"),
        P("bem", None, "fem"),
    )
    return jax.shard_map(
        per_device,
        mesh=mesh,
        in_specs=placed,
        out_specs=(P(None, ("fem", "bem")), P("bem", None, "fem")),
        check_vma=False,
    )
```

```python
import functools

import jax
import jax.numpy as jnp
from jax import lax
from jax.experimental import pallas as pl
from jax.experimental.pallas import tpu as pltpu
from jax.sharding import PartitionSpec as P

ELEM_BLOCK = 4096
ROW_BLOCK = 8192
SHARE_ROWS = (0, 3)
SHARE_COUPLING = (3, 1)
SHARE_FLUX = (4, 2)
SHARE_BACK = (6, 2)
bf16 = jnp.bfloat16
f32 = jnp.float32
i32 = jnp.int32
MESH = pl.DeviceIdType.MESH
NT = (((1,), (1,)), ((), ()))
VMEM_LIMIT = 63 << 20


def iota(shape, dim):
    return lax.broadcasted_iota(i32, shape, dim)


def to_bf(x):
    return x.astype(f32).astype(bf16)


def onehot(rows, index):
    shape = (rows, index.shape[1])
    return jnp.where(
        to_bf(iota(shape, 0)) == jnp.broadcast_to(index, shape),
        jnp.ones((), bf16),
        jnp.zeros((), bf16),
    )


def split8(x):
    hi = x.astype(bf16).astype(f32)
    return jnp.where(iota(x.shape, 0) < 4, hi, x - hi)


def split_table(t):
    hi = t.astype(bf16)
    return jnp.concatenate([hi, (t - hi.astype(f32)).astype(bf16)], 1)


def pick(table, hot, q, groups):
    r = jnp.dot(table, jnp.concatenate([hot, hot], 0), preferred_element_type=f32)
    shape = (8, hot.shape[1])
    qh = jnp.broadcast_to(q, shape) - jnp.where(iota(shape, 0) >= 4, 1, 0)
    acc = jnp.where(qh == 0, r[0:8], 0.0)
    for j in range(1, groups):
        acc = jnp.where(qh == 2 * j, r[8 * j : 8 * j + 8], acc)
    return acc + pltpu.roll(acc, 4, axis=0)


def spread(part, q, groups):
    part = part.astype(bf16)
    p16 = jnp.concatenate([part, part], 0)
    qv = to_bf(jnp.broadcast_to(q, p16.shape) - jnp.where(iota(p16.shape, 0) >= 8, 1, 0))
    zero = jnp.zeros((), bf16)
    return jnp.concatenate(
        [jnp.where(qv == jnp.asarray(2 * j, bf16), p16, zero) for j in range(groups)], 0
    )


def elem_blocks(table, mats_ref, nodes_ref, out_ref, first, blocks):
    @pl.loop(first, first + blocks)
    def _(i):
        at = pl.ds(pl.multiple_of(i * ELEM_BLOCK, ELEM_BLOCK), ELEM_BLOCK)
        nodes = nodes_ref[:, at]
        hots, xs = [], []
        for a in range(4):
            n = nodes[a : a + 1]
            hot = onehot(256, to_bf(n & 255))
            hots.append(hot)
            xs.append(pick(table[...], hot, n >> 8, 18))
        total = None
        for b in range(4):
            c = mats_ref[0, pl.ds(b, 1), at] * xs[0]
            for a in range(1, 4):
                c = c + mats_ref[a, pl.ds(b, 1), at] * xs[a]
            d = lax.dot_general(
                spread(split8(c), (nodes[b : b + 1] >> 8) - 2, 16),
                hots[b],
                NT,
                preferred_element_type=f32,
            )
            total = d if total is None else total + d
        out_ref[...] += total


def coded(exponent, mantissa, negative):
    size = ((mantissa + 128) << exponent).astype(f32)
    return jnp.where(negative, -size, size)


def bucket_rows(count_ref, node_ref, block_ref, pos_ref, weight_ref, out_ref, acc, meanwhile):
    rb = ROW_BLOCK
    acc[...] = jnp.zeros_like(acc)

    def step(i, before):
        meanwhile(i)
        at = pl.ds(pl.multiple_of(i * rb, rb), rb)
        node, pos, block = node_ref[:, at], pos_ref[:, at], block_ref[:, at]
        row = i * rb + iota((1, rb), 1)
        coef = jnp.where(row < count_ref[0], weight_ref[:, at], 0.0)
        bucket = (block & 7) * 16 + (block >> 3)

        owner = onehot(128, to_bf(bucket))
        upper = jnp.where(iota((256, 256), 0) <= iota((256, 256), 1), 1.0, 0.0).astype(bf16)
        ranks = []
        for k in range(0, rb, 256):
            hot = owner[:, k : k + 256]
            counts = jnp.dot(hot, upper, preferred_element_type=f32) + before
            ranks.append(jnp.sum(hot.astype(f32) * counts, axis=0, keepdims=True) - 1.0)
            before = counts[:, 255:256]
        slot = onehot(256, jnp.concatenate(ranks, 1).astype(bf16))

        hi = coef.astype(bf16).astype(f32)
        first = coded(pos >> 7, pos & 127, (node & 4096) > 0)
        second = coded((node >> 7) & 15, node & 127, (node & 2048) > 0)
        sub = iota((16, rb), 0) & 3
        part = jnp.broadcast_to(coef - hi, (16, rb))
        for k, item in enumerate((first, second, hi)):
            part = jnp.where(sub == k, jnp.broadcast_to(item, (16, rb)), part)
        part = part.astype(bf16)
        at16 = to_bf(jnp.broadcast_to(bucket, (16, rb)) - (iota((16, rb), 0) >> 2))
        zero = jnp.zeros((), bf16)
        spread4 = jnp.concatenate(
            [jnp.where(at16 == jnp.asarray(4 * j, bf16), part, zero) for j in range(32)], 0
        )
        acc[...] += lax.dot_general(spread4, slot, NT, preferred_element_type=f32)
        return before

    lax.fori_loop(0, node_ref.shape[1] // rb, step, jnp.zeros((128, 1), f32))

    rows = 64

    @pl.loop(0, 512 // rows)
    def _(i):
        v = acc[pl.ds(pl.multiple_of(i * rows, rows), rows), :]
        size = jnp.abs(v)
        sign = jnp.where(v < 0, 1.0, 0.0)
        e = jnp.zeros(v.shape, i32)
        for k in range(1, 16):
            e = e + jnp.where(size >= 128.0 * 2**k, 1, 0)
        code = ((e << 7) + (size.astype(i32) >> e) - 128).astype(f32)
        kind = iota(v.shape, 0) & 3
        node = code + 2048.0 * sign + 4096.0 * pltpu.roll(sign, 1, axis=0)
        coef = v + pltpu.roll(v, rows - 1, axis=0)
        out = jnp.where(kind == 0, code, jnp.where(kind == 1, node, coef))
        for j in range(rows // 8):
            tile = out[8 * j : 8 * j + 8]
            out_ref[i * (rows // 4) + 2 * j] = tile
            out_ref[i * (rows // 4) + 2 * j + 1] = pltpu.roll(tile, 4, axis=0)


DEVICES = 128


def place(index):
    wide = lax.axis_size("bem")
    return (index // wide, lax.rem(index, wide))


def greet(me, first, count):
    barrier = pltpu.get_barrier_semaphore()
    for k in range(count):
        peer = lax.rem(me + first + k, DEVICES)
        pl.semaphore_signal(barrier, inc=1, device_id=place(peer), device_id_type=MESH)


def await_all():
    pl.semaphore_wait(pltpu.get_barrier_semaphore(), DEVICES - 1)


def remote(src, dst, sems, at, device):
    return pltpu.make_async_remote_copy(
        src_ref=src,
        dst_ref=dst,
        send_sem=sems.at[at],
        recv_sem=sems.at[at + 1],
        device_id=device,
        device_id_type=MESH,
    )


def wait_bytes(ref, sem):
    pltpu.make_async_copy(ref, ref, sem).wait()


def send_chunks(me, send, got, sems, at, fill):
    group = 32

    def chunk(i, last):
        peers = [lax.rem(me + i * group + j + 1, DEVICES) for j in range(group)]
        fill(peers)
        for peer in peers[: group - 1] if last else peers:
            remote(send.at[peer], got.at[me], sems, at, place(peer)).start()

    @pl.loop(0, DEVICES // group - 1)
    def _(i):
        chunk(i, False)

    chunk(DEVICES // group - 1, True)
    got[me] = send[me]


def wait_copies(ref, count, sems, at):
    most = ref.at[pl.ds(0, count - 1)]
    wait_bytes(most, sems.at[at])
    wait_bytes(most, sems.at[at + 1])


def sum_rows(got, left, near, acc, near_out, part_ref):
    acc[...] = jnp.zeros_like(acc)
    group = 32

    @pl.loop(0, DEVICES // group)
    def _(i):
        tiles = [got[i * group + j] for j in range(group)]
        vals = jnp.concatenate([t[0:4] for t in tiles], 1)
        pos = jnp.concatenate([t[4:5] for t in tiles], 1).astype(i32)
        acc[...] += lax.dot_general(
            spread(split8(jnp.concatenate([vals, vals], 0)), pos >> 7, 5),
            onehot(128, to_bf(pos & 127)),
            NT,
            preferred_element_type=f32,
        )

    pieces = []
    for t in range(9):
        a = acc[8 * t : 8 * t + 8]
        piece = split8(a + pltpu.roll(a, 4, axis=0)).astype(bf16)
        pieces.append(piece)
        n = jnp.dot(piece, near[t], preferred_element_type=f32)
        near_out[:, 128 * t : 128 * t + 128] = (n + pltpu.roll(n, 4, axis=0))[0:4]
    c = lax.dot_general(jnp.concatenate(pieces, 1), left[...], NT, preferred_element_type=f32)
    part_ref[...] = (c + pltpu.roll(c, 4, axis=0))[0:4]


def far_field(parts, right, shares):
    total = parts[0]
    for k in range(1, parts.shape[0]):
        total = total + parts[k]
    for half in range(2):
        c = total[:, 256 * half : 256 * half + 256]
        c = split8(jnp.concatenate([c, c], 0))
        stacked = jnp.concatenate([c] * 8, 0)
        shape = stacked.shape
        diag = jnp.where((iota(shape, 0) >> 3) == (iota(shape, 1) >> 5), stacked, 0.0).astype(bf16)
        far = jnp.dot(diag, right[256 * half : 256 * half + 256], preferred_element_type=f32)
        for s in range(8):
            a = far[8 * s : 8 * s + 8]
            shares[8 * half + s] = (a + pltpu.roll(a, 4, axis=0))[0:4]


def add_returned(got, slots, acc):
    group = 32

    @pl.loop(0, DEVICES // group)
    def _(i):
        at = [i * group + j for j in range(group)]
        node = jnp.concatenate([slots[s, 1:2] for s in at], 1).astype(i32)
        coef = jnp.concatenate([slots[s, 2:3] for s in at], 1)
        x = jnp.concatenate([got[s] for s in at], 1)
        x = jnp.concatenate([x, x], 0) * coef
        acc[...] += lax.dot_general(
            spread(split8(x), node >> 8, 16),
            onehot(256, to_bf(node & 255)),
            NT,
            preferred_element_type=f32,
        )


def whole_kernel(
    count_ref,
    field_hbm,
    node_hbm,
    block_hbm,
    pos_hbm,
    weight_hbm,
    bem_hbm,
    mats_hbm,
    nodes_hbm,
    left_hbm,
    near_hbm,
    right_hbm,
    stiff,
    flux_out,
    field,
    node_ref,
    block_ref,
    pos_ref,
    weight_ref,
    bem_ref,
    field_ref,
    mats,
    nodes,
    left,
    near,
    right,
    bucket_acc,
    slots,
    table,
    own,
    halo,
    send,
    got,
    row_acc,
    part_ref,
    near_out,
    parts,
    shares,
    sums,
    flux_f32,
    flux_table,
    send_back,
    got_back,
    sems,
    local_sems,
):
    fems, bems = lax.axis_size("fem"), lax.axis_size("bem")
    f, b = lax.axis_index("fem"), lax.axis_index("bem")
    me = f * bems + b
    pairs = [
        (block_hbm, block_ref),
        (node_hbm, node_ref),
        (pos_hbm, pos_ref),
        (weight_hbm, weight_ref),
        (field_hbm, field),
        (nodes_hbm, nodes),
        (mats_hbm, mats),
        (left_hbm, left),
        (near_hbm, near),
        (right_hbm, right),
        (bem_hbm, bem_ref),
    ]
    loads = [
        pltpu.make_async_copy(src, dst, local_sems.at[k]) for k, (src, dst) in enumerate(pairs)
    ]
    for load in loads:
        load.start()
    greet(me, 1, 7)
    stiff[...] = jnp.zeros_like(stiff)
    for load in loads[:4]:
        load.wait()
    steps = node_ref.shape[1] // ROW_BLOCK
    share = (DEVICES - 8) // steps
    bucket_rows(
        count_ref,
        node_ref,
        block_ref,
        pos_ref,
        weight_ref,
        slots,
        bucket_acc,
        lambda i: greet(me, 8 + i * share, share),
    )
    loads[4].wait()
    for q in range(32):
        field_ref[4 * q : 4 * q + 4] = field[:, 256 * q : 256 * q + 256]
    own[...] = split_table(field_ref[...])

    await_all()
    up = remote(
        field_ref.at[pl.ds(120, 8)], halo.at[0], sems, 0, place(lax.rem(me + 1, DEVICES))
    )
    down = remote(
        field_ref.at[pl.ds(0, 8)], halo.at[1], sems, 2, place(lax.rem(me + DEVICES - 1, DEVICES))
    )
    up.start()
    down.start()

    def fill_rows(peers):
        parts8 = [slots[p] for p in peers]
        node = jnp.concatenate([t[1:2] for t in parts8], 1).astype(i32)
        coef = jnp.concatenate([t[2:3] for t in parts8], 1)
        x = pick(own[...], onehot(256, to_bf(node & 255)), node >> 8, 16) * coef
        for j, p in enumerate(peers):
            send[p, 0:4] = x[0:4, 256 * j : 256 * j + 256]
            send[p, 4:5] = parts8[j][0:1]

    send_chunks(me, send, got, sems, 4, fill_rows)

    up.wait()
    down.wait()
    table[0:8] = split_table(jnp.where(me == 0, 0.0, halo[0]))
    table[8:136] = own[...]
    table[136:144] = split_table(jnp.where(me == DEVICES - 1, 0.0, halo[1]))
    loads[5].wait()
    loads[6].wait()
    elem_blocks(table, mats, nodes, stiff, *SHARE_ROWS)
    wait_copies(got, DEVICES, sems, 4)

    loads[7].wait()
    loads[8].wait()
    sum_rows(got, left, near, row_acc, near_out, part_ref)
    for k in range(1, fems):
        remote(part_ref, parts.at[f], sems, 6, (lax.rem(f + k, fems), b)).start()
    parts[f] = part_ref[...]
    elem_blocks(table, mats, nodes, stiff, *SHARE_COUPLING)
    wait_copies(parts, fems, sems, 6)

    loads[9].wait()
    far_field(parts, right, shares)
    shares[b] = shares[b] + near_out[...]
    for k in range(1, bems):
        peer = lax.rem(b + k, bems)
        remote(shares.at[peer], sums.at[b], sems, 8, (f, peer)).start()
    sums[b] = shares[b]
    elem_blocks(table, mats, nodes, stiff, *SHARE_FLUX)
    wait_copies(sums, bems, sems, 8)

    loads[10].wait()
    flux = bem_ref[...]
    for k in range(bems):
        flux = flux + sums[k]
    flux_out[...] = flux
    flux_f32[...] = jnp.zeros_like(flux_f32)
    for t in range(9):
        flux_f32[4 * t : 4 * t + 4] = flux[:, 128 * t : 128 * t + 128]
    flux_table[...] = split_table(flux_f32[...])

    def fill_back(peers):
        pos = jnp.concatenate([got[p, 4:5] for p in peers], 1).astype(i32)
        x = pick(flux_table[...], onehot(128, to_bf(pos & 127)), pos >> 7, 5)
        for j, p in enumerate(peers):
            send_back[p] = x[0:4, 256 * j : 256 * j + 256]

    send_chunks(me, send_back, got_back, sems, 10, fill_back)
    elem_blocks(table, mats, nodes, stiff, *SHARE_BACK)
    wait_copies(got_back, DEVICES, sems, 10)

    add_returned(got_back, slots, stiff)


def whole_call(*args):
    vmem = pl.BlockSpec(memory_space=pltpu.VMEM)
    hbm = pl.BlockSpec(memory_space=pl.ANY)
    rows, elems = args[2].shape[1], args[8].shape[1]
    return pl.pallas_call(
        whole_kernel,
        in_specs=[pl.BlockSpec(memory_space=pltpu.SMEM)] + [hbm] * 11,
        out_specs=[vmem] * 2,
        out_shape=[jax.ShapeDtypeStruct((256, 256), f32), jax.ShapeDtypeStruct((4, 1152), f32)],
        scratch_shapes=[
            pltpu.VMEM((4, 8192), f32),
            pltpu.VMEM((1, rows), i32),
            pltpu.VMEM((1, rows), i32),
            pltpu.VMEM((1, rows), i32),
            pltpu.VMEM((1, rows), f32),
            pltpu.VMEM((4, 1152), f32),
            pltpu.VMEM((128, 256), f32),
            pltpu.VMEM((4, 4, elems), f32),
            pltpu.VMEM((4, elems), i32),
            pltpu.VMEM((512, 1152), bf16),
            pltpu.VMEM((9, 128, 128), bf16),
            pltpu.VMEM((512, 1152), bf16),
            pltpu.VMEM((512, 256), f32),
            pltpu.VMEM((DEVICES, 8, 256), f32),
            pltpu.VMEM((144, 512), bf16),
            pltpu.VMEM((128, 512), bf16),
            pltpu.VMEM((2, 8, 256), f32),
            pltpu.VMEM((DEVICES, 5, 256), f32),
            pltpu.VMEM((DEVICES, 5, 256), f32),
            pltpu.VMEM((80, 128), f32),
            pltpu.VMEM((4, 512), f32),
            pltpu.VMEM((4, 1152), f32),
            pltpu.VMEM((8, 4, 512), f32),
            pltpu.VMEM((16, 4, 1152), f32),
            pltpu.VMEM((16, 4, 1152), f32),
            pltpu.VMEM((40, 128), f32),
            pltpu.VMEM((40, 256), bf16),
            pltpu.VMEM((DEVICES, 4, 256), f32),
            pltpu.VMEM((DEVICES, 4, 256), f32),
            pltpu.SemaphoreType.DMA((12,)),
            pltpu.SemaphoreType.DMA((11,)),
        ],
        compiler_params=pltpu.CompilerParams(
            collective_id=0, has_side_effects=True, vmem_limit_bytes=VMEM_LIMIT
        ),
        name="whole",
    )(*args)


def finish_kernel(parts_ref, flux_ref, fem_out, flux_out):
    flux_out[0] = flux_ref[...]
    for q in range(32):
        a = parts_ref[8 * q : 8 * q + 8]
        fem_out[:, 256 * q : 256 * q + 256] = (a + pltpu.roll(a, 4, axis=0))[0:4]


def finish_call(parts, flux):
    vmem = pl.BlockSpec(memory_space=pltpu.VMEM)
    return pl.pallas_call(
        finish_kernel,
        in_specs=[vmem] * 2,
        out_specs=[vmem] * 2,
        out_shape=[jax.ShapeDtypeStruct((4, 8192), f32), jax.ShapeDtypeStruct((1, 4, 1152), f32)],
        compiler_params=pltpu.CompilerParams(vmem_limit_bytes=VMEM_LIMIT),
        name="finish",
    )(parts, flux)


def per_device(
    fem_field,
    elem_mats,
    elem_nodes,
    trace_count,
    trace_node,
    trace_block,
    trace_pos,
    trace_weight,
    near_tiles,
    left_basis,
    right_basis,
    bem_field,
):
    parts, flux = whole_call(
        trace_count,
        fem_field,
        trace_node.reshape(1, -1),
        trace_block.reshape(1, -1),
        trace_pos.reshape(1, -1),
        trace_weight.reshape(1, -1),
        bem_field[0],
        elem_mats,
        elem_nodes,
        left_basis.reshape(512, 1152),
        near_tiles[0],
        right_basis.reshape(512, 1152),
    )
    return finish_call(parts, flux)


def solution(mesh):
    placed = (
        P(None, ("fem", "bem")),
        P(None, None, ("fem", "bem")),
        P(None, ("fem", "bem")),
        P(("fem", "bem")),
        P(("fem", "bem")),
        P(("fem", "bem"), None),
        P(("fem", "bem")),
        P(("fem", "bem")),
        P("bem", "fem", None, None),
        P("bem", None, None, "fem"),
        P("bem", None, None, "fem"),
        P("bem", None, "fem"),
    )
    return jax.shard_map(
        per_device,
        mesh=mesh,
        in_specs=placed,
        out_specs=(P(None, ("fem", "bem")), P("bem", None, "fem")),
        check_vma=False,
    )
```
